256 devices in a mesh: row: 16 (over y, x), col: 16 (over z, core).
Axes of the slice: x: 4, y: 4, z: 8, core: 2. Of those that a mesh axis runs over, the one named last changes fastest.
Arguments:
- targets: float32 [2, 131072], P(None, ('row', 'col')), may hold values from 0 to 1
- sources: bfloat16 [2, 32768], P(None, 'col'), may hold values from 0 to 1
- omega: bfloat16 [256, 32768], P(None, 'col'), may hold values from -0.03125 to 0.03125
- tree_order: int32 [131072], P(('row', 'col')), may hold values from 0 to 131071, each once
- leaf_pivots: int32 [256, 128], P(('row', 'col')), may hold values from 0 to 511, all different within a row
- pivots_one: int32 [128, 128], replicated, may hold values from 0 to 255, all different within a row
- pivots_two: int32 [64, 128], replicated, may hold values from 0 to 255, all different within a row
- pivots_three: int32 [32, 128], replicated, may hold values from 0 to 255, all different within a row
Outputs:
- leaf_interp: float32 [131072, 128], P(('row', 'col'))
- level_one_interp: float32 [32768, 128], P(('row', 'col'))
- level_two_interp: float32 [16384, 128], P(('row', 'col'))
- level_three_interp: float32 [8192, 128], P(('row', 'col'))
- root_sketch: float32 [4096, 256], P(('row', 'col'))
The draws below stay inside these ranges and needn't reach their ends.
Inputs may be any that keep to these rules, and one draw needn't show every extreme that they name: tree_order names every target point once. `leaf_pivots`: each row names 128 distinct positions. `pivots_one`: each row names 128 distinct positions. `pivots_two`: each row names 128 distinct positions. `pivots_three`: each row names 128 distinct positions.
All inputs are finite; a program needn't handle non-finite values.
Results may differ from the reference program's by a relative error of at most 0.0074.
Values may be sent and summed in bfloat16 or wider, within the bound.
No kernel may reach another device: no remote copies, remote signals or barrier semaphores. Data moves between devices by JAX's collectives and lax.ppermute only.
A program may use at most 192 MiB of HBM per device.

```python
import jax
import jax.numpy as jnp
from jax import lax

LEAF = 512
K = 128
S = 256
N = 131072
P_SIZE = 32768
NODES1 = 128
NODES2 = 64
NODES3 = 32


def level_of(own_key, extent, cuts, low, largest):
    def one(dim, blocks):
        heights = jax.random.uniform(jax.random.fold_in(jax.random.fold_in(own_key, 6), dim), (blocks,), jnp.float32, low / len(cuts), largest / len(cuts))
        return jnp.repeat(jnp.exp(heights), extent[dim] // blocks).reshape((-1,) + (1,) * (len(extent) - dim - 1))

    loudness = one(*cuts[0])
    for cut in cuts[1:]:
        loudness = loudness * one(*cut)
    return loudness


def choose_distinct(stream_key, rows, amount, top, lift):
    ranking = jax.random.permutation(jax.random.fold_in(stream_key, 1), amount)
    favour = ranking
    for power in range(3):
        favour = favour * favour // amount
    favour = favour * lift // amount
    chance = jax.random.randint(jax.random.fold_in(stream_key, 2), (rows, amount), 0, 4096) + favour
    sure = jax.random.permutation(jax.random.fold_in(stream_key, 3), rows)[jnp.arange(amount) % rows]
    chance = jnp.where(jnp.arange(rows)[:, None] == sure[None, :], 1 << 14, chance)
    priority = chance * amount + jnp.arange(amount)
    return lax.top_k(priority.astype(jnp.int32), top)[1].astype(jnp.int32)


def bell_draw(stream_key, dims, deviation, bound, cuts=(), held_as=jnp.bfloat16):
    array = jax.random.normal(stream_key, dims, jnp.float32) * deviation
    if len(cuts) > 0:
        array = level_of(stream_key, dims, cuts, -0.22, 0.18) * array
    return jnp.clip(array, min=-bound, max=bound).astype(held_as)


def setup_inputs(seed: int = 0) -> dict:
    key_of = jax.random.split(jax.random.key(seed), 9)
    targets = jnp.clip(1.0 * jax.random.uniform(key_of[0], (2, N), jnp.float32) ** level_of(key_of[0], (2, N), ((1, 256),), -0.2, 0.2), 0.0, 1.0)
    sources = jnp.clip(1.0 * jax.random.uniform(key_of[1], (2, P_SIZE), jnp.float32) ** level_of(key_of[1], (2, P_SIZE), ((1, 16),), -0.2, 0.2), 0.0, 1.0).astype(jnp.bfloat16)
    omega = bell_draw(key_of[2], (S, P_SIZE), P_SIZE ** -0.5, 0.03125, ((1, 16),))
    tree_order = jax.random.permutation(key_of[3], N).astype(jnp.int32)
    leaf_pivots = choose_distinct(key_of[4], (N // LEAF), LEAF, K, 0)
    pivots_one = choose_distinct(key_of[5], NODES1, 2 * K, K, 0)
    pivots_two = choose_distinct(key_of[6], NODES2, 2 * K, K, 0)
    pivots_three = choose_distinct(key_of[7], NODES3, 2 * K, K, 0)
    return {"targets": targets, "sources": sources, "omega": omega, "tree_order": tree_order, "leaf_pivots": leaf_pivots, "pivots_one": pivots_one, "pivots_two": pivots_two, "pivots_three": pivots_three}


RIDGE = 0.1
DELTA_SQUARED = 0.0001

def kernel_block(points, source_pts):
    delta_x = points[0][:, None] - source_pts[0][None, :].astype(jnp.float32)
    delta_y = points[1][:, None] - source_pts[1][None, :].astype(jnp.float32)
    return (-0.5 * jnp.log(delta_x * delta_x + delta_y * delta_y + DELTA_SQUARED)).astype(jnp.bfloat16)

def select_factor(candidates, pivots):
    chosen = jnp.take(candidates, pivots, axis=0)
    gram_matrix = jnp.dot(chosen, chosen.T, precision=lax.Precision.HIGHEST)
    ridge_shift = RIDGE * (jnp.trace(gram_matrix) / chosen.shape[0] + 1e-06)
    shifted = gram_matrix + ridge_shift * jnp.eye(chosen.shape[0], dtype=gram_matrix.dtype)
    return (chosen, jnp.linalg.cholesky(shifted))

def solve_rows(chosen, factor, row_block):
    right_side = jnp.dot(chosen, row_block.T, precision=lax.Precision.HIGHEST)
    first = lax.linalg.triangular_solve(factor, right_side, left_side=True, lower=True)
    second = lax.linalg.triangular_solve(factor, first, left_side=True, lower=True, transpose_a=True)
    return second.T

def reference(targets, sources, omega, tree_order, leaf_pivots, pivots_one, pivots_two, pivots_three):
    placed = jnp.take(targets, tree_order, axis=1)
    blocks = placed.reshape(2, N // LEAF, LEAF).transpose(1, 0, 2)

    def sketch_block(block):
        panel = kernel_block(block, sources)
        return lax.dot_general(panel.astype(jnp.float32), omega.astype(jnp.float32), (((1,), (1,)), ((), ())), preferred_element_type=jnp.float32)
    leaf_sketches = lax.map(sketch_block, blocks)
    chosen, factors = jax.vmap(select_factor)(leaf_sketches, leaf_pivots)
    results = [jax.vmap(solve_rows)(chosen, factors, leaf_sketches).reshape(N, K)]
    for pivot_table in (pivots_one, pivots_two, pivots_three):
        candidates = chosen.reshape(-1, 2 * K, S)
        chosen, factors = jax.vmap(select_factor)(candidates, pivot_table)
        results.append(jax.vmap(solve_rows)(chosen, factors, candidates).reshape(-1, K))
    return (results[0], results[1], results[2], results[3], chosen.reshape(-1, S))
```

```python
import functools

import jax
import jax.numpy as jnp
from jax import lax
from jax.experimental import pallas as pl
from jax.experimental.pallas import tpu as pltpu
from jax.sharding import Mesh
from jax.sharding import PartitionSpec as P

LEAF = 512
S = 256
K = 128
FEATURES = 16
PIECE = 16
RIDGE = 0.1
DELTA_SQUARED = 0.0001
ALL_AXES = ("y", "x", "z", "k")
NY, NX, NZ, NK = 4, 4, 8, 2
STEPS = (2, -1, 1)
F32 = jnp.float32
BF16 = jnp.bfloat16
VMEM_LIMIT = 40 << 20


def params():
    return pltpu.CompilerParams(vmem_limit_bytes=VMEM_LIMIT)


def smem():
    return pl.BlockSpec(memory_space=pltpu.SMEM)


def vmem():
    return pl.BlockSpec(memory_space=pltpu.VMEM)


def split3(value):
    high = value.astype(BF16).astype(F32)
    rest = value - high
    middle = rest.astype(BF16).astype(F32)
    low = (rest - middle).astype(BF16).astype(F32)
    return high, middle, low


def lookup_kernel(place_ref, table_ref, *refs):
    lists, outs = refs[:8], refs[8:]
    y, x, z, k = place_ref[0], place_ref[1], place_ref[2], place_ref[3]
    tables = []
    for coord in range(2):
        turned = jnp.transpose(table_ref[coord])
        tables.append(jnp.concatenate([part.astype(BF16) for part in split3(turned)], axis=1))
    line = lax.broadcasted_iota(jnp.int32, (128, LEAF), 0)
    for index_ref, out_ref in zip(lists, outs):
        index = index_ref[...]
        owner = index >> 9
        own_k, own_z, own_x, own_y = owner & 1, (owner >> 1) & 7, (owner >> 4) & 3, owner >> 6
        row = (((x - own_x) & 3) * 8 + ((z - own_z) & 7)) * 4 + ((index >> 7) & 3)
        row = jnp.where(jnp.logical_and(own_y == y, own_k == k), row, -1)
        hot = jnp.where(line == row, 1.0, 0.0).astype(BF16)
        hot = jnp.concatenate([hot, hot, hot], axis=0)
        mask = line == (index & 127)
        found = []
        for coord in range(2):
            rows = jnp.dot(tables[coord], hot, preferred_element_type=F32)
            found.append(jnp.sum(jnp.where(mask, rows, 0.0), axis=0, keepdims=True))
        out_ref[...] = jnp.concatenate(found, axis=0)


def placed_points(targets, tree_order, y, x, z, k):
    order = tree_order.reshape(1, LEAF)
    yk = [(dy, dk) for dy in range(NY) for dk in range(NK)]

    def route(dy, dk):
        return [
            (sy * NK + sk, (sy + dy) % NY * NK + (sk ^ dk)) for sy in range(NY) for sk in range(NK)
        ]

    lists = [
        lax.ppermute(order, ("y", "k"), route(dy, dk)) if (dy, dk) != (0, 0) else order
        for dy, dk in yk
    ]
    own = targets.reshape(2, 1, 4, 128)
    planes = [own] + [
        lax.ppermute(own, "z", [(s, (s + step) % NZ) for s in range(NZ)]) for step in range(1, NZ)
    ]
    table = jnp.concatenate(planes, axis=1)
    lines = [table] + [
        lax.ppermute(table, "x", [(s, (s + step) % NX) for s in range(NX)]) for step in range(1, NX)
    ]
    table = jnp.concatenate(lines, axis=1).reshape(2, 128, 128)
    place = jnp.stack([y, x, z, k]).astype(jnp.int32)
    found = pl.pallas_call(
        lookup_kernel,
        out_shape=[jax.ShapeDtypeStruct((2, LEAF), F32)] * 8,
        in_specs=[smem()] + [vmem()] * 9,
        out_specs=[vmem()] * 8,
        compiler_params=params(),
        name="lookup",
    )(place, table, *lists)
    total = found[0]
    for (dy, dk), part in zip(yk[1:], found[1:]):
        total = total + lax.ppermute(part, ("y", "k"), route(-dy % NY, dk))
    return total


def source_kernel(*refs):
    for source_ref, out_ref in zip(refs[:4], refs[4:]):
        points = source_ref[...].astype(F32)
        sx, sy = points[0:1], points[1:2]
        size = split3(sx * sx + sy * sy)
        one = jnp.ones_like(sx)
        zero = jnp.zeros_like(sx)
        rows = [-2.0 * sx] * 3 + [-2.0 * sy] * 3 + [one] * 3 + list(size) + [zero] * 4
        out_ref[...] = jnp.concatenate(rows, axis=0).astype(BF16)


def source_features(blocks):
    width = blocks[0].shape[1]
    return pl.pallas_call(
        source_kernel,
        out_shape=[jax.ShapeDtypeStruct((FEATURES, width), BF16)] * 4,
        in_specs=[vmem()] * 4,
        out_specs=[vmem()] * 4,
        compiler_params=params(),
        name="source_features",
    )(*blocks)


def sketch_kernel(points_ref, *refs, chunk):
    features, weights, (out_ref, held, feat, sems) = refs[:4], refs[4:8], refs[8:]
    copies = [
        pltpu.make_async_copy(weight, held.at[i], sems.at[i]) for i, weight in enumerate(weights)
    ]
    for copy in copies:
        copy.start()
    for i in range(4):
        feat[i] = features[i][...]
    points = points_ref[...]
    tx, ty = points[0:1], points[1:2]
    one = jnp.ones_like(tx)
    zero = jnp.zeros_like(tx)
    size = split3(tx * tx + (ty * ty + DELTA_SQUARED))
    rows = list(split3(tx)) + list(split3(ty)) + list(size) + [one] * 3 + [zero] * 4
    target = jnp.transpose(jnp.concatenate(rows, axis=0)).astype(BF16)
    out_ref[...] = jnp.zeros_like(out_ref)
    width = held.shape[2]
    for i in range(4):
        copies[i].wait()
        total = out_ref[...]
        for j in range(width // chunk):
            span = slice(j * chunk, (j + 1) * chunk)
            squared = jnp.dot(target, feat[i, :, span], preferred_element_type=F32)
            panel = jnp.log(squared).astype(BF16)
            total = total + lax.dot_general(
                panel, held[i, :, span], (((1,), (1,)), ((), ())), preferred_element_type=F32
            )
        out_ref[...] = total * (-0.5) if i == 3 else total


def sketch_part(points, features, weights):
    count = points.shape[1]
    width = weights[0].shape[1]
    return pl.pallas_call(
        functools.partial(sketch_kernel, chunk=256),
        out_shape=jax.ShapeDtypeStruct((count, S), F32),
        in_specs=[vmem()] * 5 + [pl.BlockSpec(memory_space=pl.ANY)] * 4,
        out_specs=vmem(),
        scratch_shapes=[
            pltpu.VMEM((4, S, width), BF16),
            pltpu.VMEM((4, FEATURES, width), BF16),
            pltpu.SemaphoreType.DMA((4,)),
        ],
        compiler_params=params(),
        name="sketch",
    )(points, *features, *weights)


def assemble_kernel(spot_ref, *refs):
    parts, out_ref, sems = refs[:4], refs[4], refs[5]
    copies = []
    for b in range(4):
        for a in range(4):
            start = pl.multiple_of(spot_ref[4 * b + a], PIECE)
            copies.append(
                pltpu.make_async_copy(
                    parts[b].at[a], out_ref.at[pl.ds(start, PIECE)], sems.at[4 * b + a]
                )
            )
    for copy in copies:
        copy.start()
    for copy in copies:
        copy.wait()


def swap_cores(value):
    return lax.ppermute(value, "k", [(0, 1), (1, 0)])


def far_block(omega, y, x, k):
    piece = lax.dynamic_slice_in_dim(omega, (y * NX + x) * PIECE, PIECE, 0)
    piece = lax.ppermute(piece, "z", [(s, (s + 4) % NZ) for s in range(NZ)])[None]

    def turn(step, x_core):
        pairs = []
        for sy in range(NY):
            for sx in range(NX):
                for sk in range(NK):
                    ty, tx = (sy, (sx + step) % NX) if sk == x_core else ((sy + step) % NY, sx)
                    pairs.append(((sy * NX + sx) * NK + sk, (ty * NX + tx) * NK + sk))
        return pairs

    group = ("y", "x", "k")
    line = jnp.concatenate(
        [piece] + [lax.ppermute(piece, group, turn(step, 0)) for step in range(1, 4)], axis=0
    )
    lines = [line] + [lax.ppermute(line, group, turn(step, 1)) for step in range(1, 4)]
    b, a = jnp.arange(16, dtype=jnp.int32) // 4, jnp.arange(16, dtype=jnp.int32) % 4
    dy, dx = jnp.where(k == 0, b, a), jnp.where(k == 0, a, b)
    spots = ((((y - dy) & 3) * 4 + ((x - dx) & 3)) * PIECE).astype(jnp.int32)
    return pl.pallas_call(
        assemble_kernel,
        out_shape=jax.ShapeDtypeStruct(omega.shape, BF16),
        in_specs=[smem()] + [pl.BlockSpec(memory_space=pl.ANY)] * 4,
        out_specs=pl.BlockSpec(memory_space=pl.ANY),
        scratch_shapes=[pltpu.SemaphoreType.DMA((16,))],
        compiler_params=params(),
        name="assemble",
    )(spots, *lines)


def along_z(step, forward):
    pairs = []
    for sz in range(NZ):
        for sk in range(NK):
            move = step if (sk == 0) == forward else -step
            pairs.append((sz * NK + sk, (sz + move) % NZ * NK + sk))
    return pairs


def take_rows(pivot_ref, source_ref, out_ref):
    def body(step, carry):
        for i in range(8):
            spot = step * 8 + i
            out_ref[pl.ds(spot, 1), :] = source_ref[pl.ds(pivot_ref[spot], 1), :]
        return carry

    lax.fori_loop(0, K // 8, body, 0)


def sum_kernel(pivot_ref, low_ref, high_ref, a_ref, b_ref, c_ref, out_ref, chosen_ref):
    half = LEAF // 2
    for part_ref, rows in ((low_ref, slice(0, half)), (high_ref, slice(half, LEAF))):
        out_ref[rows, :] = (part_ref[...] + a_ref[rows, :]) + (b_ref[rows, :] + c_ref[rows, :])
    take_rows(pivot_ref, out_ref, chosen_ref)


def choose_kernel(pivot_ref, own_ref, other_ref, chosen_ref, both):
    both[0:K, :] = own_ref[...]
    both[K:, :] = other_ref[...]
    take_rows(pivot_ref, both, chosen_ref)


def choose(pivots, own, other):
    return pl.pallas_call(
        choose_kernel,
        out_shape=jax.ShapeDtypeStruct((K, S), F32),
        in_specs=[smem(), vmem(), vmem()],
        out_specs=vmem(),
        scratch_shapes=[pltpu.VMEM((2 * K, S), F32)],
        compiler_params=params(),
        name="choose",
    )(pivots, own, other)


def eliminate(matrix, i):
    lane = lax.broadcasted_iota(jnp.int32, (1, K), 1)
    line = lax.broadcasted_iota(jnp.int32, (K, 1), 0)
    scale = 1.0 / matrix[i : i + 1, i : i + 1]
    row = (matrix[i : i + 1, :] - jnp.where(lane == i, 1.0, 0.0)) * scale
    column = matrix[:, i : i + 1] - jnp.where(line == i, 1.0, 0.0)
    return matrix - column * row


def dot_rows(left, right):
    return lax.dot_general(
        left,
        right,
        (((1,), (1,)), ((), ())),
        precision=lax.Precision.HIGHEST,
        preferred_element_type=F32,
    )


def tree_kernel(
    pivot_ref, spot_ref, sketch_ref, c0_ref, c1_ref, c2_ref, o2_ref,
    leaf_ref, one_ref, two_ref, three_ref, root_ref,
    both, c3_ref, work,
):
    both[0:K, :] = c2_ref[...]
    both[K:, :] = o2_ref[...]
    take_rows(pivot_ref, both, c3_ref)
    root_ref[...] = c3_ref[pl.ds(pl.multiple_of(spot_ref[2], 16), 16), :]
    lane = lax.broadcasted_iota(jnp.int32, (K, K), 1)
    line = lax.broadcasted_iota(jnp.int32, (K, K), 0)
    eye = lane == line
    chosen = (c0_ref, c1_ref, c2_ref, c3_ref)
    scales = []
    for level, ref in enumerate(chosen):
        rows = ref[...]
        gram = dot_rows(rows, rows)
        trace = jnp.sum(jnp.sum(jnp.where(eye, gram, 0.0), axis=1, keepdims=True), axis=0, keepdims=True)
        scale = 1.0 / (trace / K + 1e-06)
        scales.append(scale)
        work[level] = gram * scale + jnp.where(eye, RIDGE, 0.0)

    def block(step, carry):
        values = [work[level] for level in range(4)]
        for i in range(8):
            values = [eliminate(value, i) for value in values]
        for level in range(4):
            turned = pltpu.roll(values[level], K - 8, 1)
            work[level, 0 : K - 8, :] = turned[8:, :]
            work[level, K - 8 : K, :] = turned[:8, :]
        return carry

    lax.fori_loop(0, K // 8, block, 0)
    shares = (
        sketch_ref[...],
        c0_ref[...],
        c1_ref[pl.ds(pl.multiple_of(spot_ref[0], 64), 64), :],
        c2_ref[pl.ds(pl.multiple_of(spot_ref[1], 32), 32), :],
    )
    outs = (leaf_ref, one_ref, two_ref, three_ref)
    for level in range(4):
        inverse = (jnp.where(eye, 2.0, 0.0) - work[level]) * scales[level]
        right = dot_rows(shares[level], chosen[level][...])
        outs[level][...] = jnp.dot(
            right, inverse, precision=lax.Precision.HIGHEST, preferred_element_type=F32
        )


def body(targets, sources, omega, tree_order, leaf_pivots, pivots_one, pivots_two, pivots_three):
    y, x, z, k = (lax.axis_index(axis) for axis in ALL_AXES)
    leaf = ((y * NX + x) * NZ + z) * NK + k
    bits = (k, z & 1, (z >> 1) & 1)
    tables = (pivots_one, pivots_two, pivots_three)
    pivots = [
        lax.dynamic_index_in_dim(table, leaf >> level + 1, 0, keepdims=False)
        ^ (bits[level] * K).astype(jnp.int32)
        for level, table in enumerate(tables)
    ]
    zk = ("z", "k")

    far_own = lax.ppermute(sources, zk, [((s ^ 8), s) for s in range(16)])
    far_other = lax.ppermute(sources, zk, [((s ^ 9), s) for s in range(16)])
    features = source_features([sources, swap_cores(sources), far_own, far_other])
    near_omega = swap_cores(omega)
    far_omega = far_block(omega, y, x, k)
    weights = [omega, near_omega, far_omega, swap_cores(far_omega)]

    own_points = placed_points(targets, tree_order, y, x, z, k)
    others = [lax.ppermute(own_points, zk, along_z(step, False)) for step in STEPS]
    half = LEAF // 2
    low = sketch_part(own_points[:, :half], features, weights)
    received = [
        lax.ppermute(sketch_part(points, features, weights), zk, along_z(step, True))
        for step, points in zip(STEPS, others)
    ]
    high = sketch_part(own_points[:, half:], features, weights)
    sketch, c0 = pl.pallas_call(
        sum_kernel,
        out_shape=[jax.ShapeDtypeStruct((LEAF, S), F32), jax.ShapeDtypeStruct((K, S), F32)],
        in_specs=[smem()] + [vmem()] * 5,
        out_specs=[vmem()] * 2,
        compiler_params=params(),
        name="sum",
    )(leaf_pivots[0], low, high, *received)
    c1 = choose(pivots[0], c0, swap_cores(c0))
    c2 = choose(pivots[1], c1, lax.ppermute(c1, "z", [(s, s ^ 1) for s in range(NZ)]))
    other2 = lax.ppermute(c2, "z", [(s, s ^ 2) for s in range(NZ)])
    spots = jnp.stack(
        [k * 64, ((z & 1) * 2 + k) * 32, ((z & 3) * 2 + k) * 16]
    ).astype(jnp.int32)
    return pl.pallas_call(
        tree_kernel,
        out_shape=[
            jax.ShapeDtypeStruct((LEAF, K), F32),
            jax.ShapeDtypeStruct((K, K), F32),
            jax.ShapeDtypeStruct((K // 2, K), F32),
            jax.ShapeDtypeStruct((K // 4, K), F32),
            jax.ShapeDtypeStruct((K // 8, S), F32),
        ],
        in_specs=[smem()] * 2 + [vmem()] * 5,
        out_specs=[vmem()] * 5,
        scratch_shapes=[
            pltpu.VMEM((2 * K, S), F32),
            pltpu.VMEM((K, S), F32),
            pltpu.VMEM((4, K, K), F32),
        ],
        compiler_params=params(),
        name="tree",
    )(pivots[2], spots, sketch, c0, c1, c2, other2)


def solution(mesh):
    finer = Mesh(mesh.devices.reshape(NY, NX, NZ, NK), ALL_AXES)
    col = ("z", "k")
    placed = (
        P(None, ALL_AXES),
        P(None, col),
        P(None, col),
        P(ALL_AXES),
        P(ALL_AXES, None),
        P(),
        P(),
        P(),
    )
    return jax.shard_map(
        body,
        mesh=finer,
        in_specs=placed,
        out_specs=(P(ALL_AXES, None),) * 5,
        check_vma=False,
    )
```

```python
import functools

import jax
import jax.numpy as jnp
from jax import lax
from jax.experimental import pallas as pl
from jax.experimental.pallas import tpu as pltpu
from jax.sharding import Mesh
from jax.sharding import PartitionSpec as P

LEAF = 512
S = 256
K = 128
FEATURES = 16
RIDGE = 0.1
DELTA_SQUARED = 0.0001
ALL_AXES = ("y", "x", "z", "k")
ZK = ("z", "k")
NY, NX, NZ, NK = 4, 4, 8, 2
F32 = jnp.float32
BF16 = jnp.bfloat16
VMEM_LIMIT = 40 << 20


def params():
    return pltpu.CompilerParams(vmem_limit_bytes=VMEM_LIMIT)


def smem():
    return pl.BlockSpec(memory_space=pltpu.SMEM)


def vmem():
    return pl.BlockSpec(memory_space=pltpu.VMEM)


def split3(value):
    high = value.astype(BF16).astype(F32)
    rest = value - high
    middle = rest.astype(BF16).astype(F32)
    low = (rest - middle).astype(BF16).astype(F32)
    return high, middle, low


def lookup_kernel(me_ref, table_ref, *refs):
    lists, outs, (thirds,) = refs[:4], refs[4:8], refs[8:]
    for coord in range(2):
        for third, part in enumerate(split3(table_ref[coord])):
            thirds[third, :, coord * 128 : coord * 128 + 128] = part.astype(BF16)
    me = me_ref[0]
    line = lax.broadcasted_iota(jnp.int32, (LEAF, 1024), 1)
    lane = lax.broadcasted_iota(jnp.int32, (LEAF, 128), 1)
    slot = lax.broadcasted_iota(jnp.int32, (LEAF, FEATURES), 1)
    for index_ref, out_ref in zip(lists, outs):
        order = jnp.broadcast_to(index_ref[...].astype(F32), (8, LEAF))
        index = jnp.transpose(order)[:, 0:1].astype(jnp.int32)
        away = (index >> 9) ^ me
        row = (away & 1) * 4 + (away >> 6)
        row = ((row * 4 + ((away >> 4) & 3)) * 8 + ((away >> 1) & 7)) * 4 + ((index >> 7) & 3)
        hot = jnp.where(line == row, 1.0, 0.0).astype(BF16)
        rows = jnp.dot(hot, thirds[0], preferred_element_type=F32)
        for third in (1, 2):
            rows = rows + jnp.dot(hot, thirds[third], preferred_element_type=F32)
        mask = lane == (index & 127)
        tx = jnp.sum(jnp.where(mask, rows[:, :128], 0.0), axis=1, keepdims=True)
        ty = jnp.sum(jnp.where(mask, rows[:, 128:], 0.0), axis=1, keepdims=True)
        columns = list(split3(tx)) + list(split3(ty))
        columns += list(split3(tx * tx + (ty * ty + DELTA_SQUARED)))
        feature = jnp.where(slot < 12, 1.0, 0.0)
        for i, column in enumerate(columns):
            feature = jnp.where(slot == i, column, feature)
        out_ref[...] = feature.astype(BF16)


def near(value, axis, size, steps):
    parts = [value]
    for step in steps:
        parts.append(lax.ppermute(value, axis, [(s, s ^ step) for s in range(size)]))
    return jnp.concatenate(parts, axis=1)


def target_features(targets, tree_order, me):
    order = tree_order.reshape(1, LEAF)
    lists = [order] + [lax.ppermute(order, ZK, along_z(d, False)) for d in (1, 2, 3)]
    table = near(targets.reshape(2, 4, 128), "z", NZ, (1, 2, 3))
    table = near(table, "z", NZ, (4,))
    table = near(table, "x", NX, (1, 2, 3))
    table = near(table, "y", NY, (1, 2, 3))
    table = near(table, "k", NK, (1,))
    return pl.pallas_call(
        lookup_kernel,
        out_shape=[jax.ShapeDtypeStruct((LEAF, FEATURES), BF16)] * 4,
        in_specs=[smem()] + [vmem()] * 5,
        out_specs=[vmem()] * 4,
        scratch_shapes=[pltpu.VMEM((3, 1024, 256), BF16)],
        compiler_params=params(),
        name="lookup",
    )(me, table, *lists)


def source_kernel(*refs):
    half = len(refs) // 2
    for source_ref, out_ref in zip(refs[:half], refs[half:]):
        points = source_ref[...].astype(F32)
        sx, sy = points[0:1], points[1:2]
        size = split3(sx * sx + sy * sy)
        one = jnp.ones_like(sx)
        zero = jnp.zeros_like(sx)
        rows = [-2.0 * sx] * 3 + [-2.0 * sy] * 3 + list(size) + [zero] * 4
        rows = rows[:6] + [one] * 3 + rows[6:]
        out_ref[...] = jnp.concatenate(rows, axis=0).astype(BF16)


def source_features(*blocks):
    width = blocks[0].shape[1]
    return pl.pallas_call(
        source_kernel,
        grid=(1,),
        out_shape=[jax.ShapeDtypeStruct((FEATURES, width), BF16)] * len(blocks),
        in_specs=[pl.BlockSpec((16, width), lambda i: (S // 16, 0))] * len(blocks),
        out_specs=[pl.BlockSpec((FEATURES, width), lambda i: (0, 0))] * len(blocks),
        compiler_params=params(),
        name="source_features",
    )(*blocks)


def sketch_kernel(target_ref, *refs, chunk):
    features, weights, (out_ref, total_ref, held, feat, sems) = refs[:4], refs[4:8], refs[8:]
    copies = [
        pltpu.make_async_copy(weight.at[pl.ds(0, S)], held.at[i], sems.at[i])
        for i, weight in enumerate(weights)
    ]
    for copy in copies:
        copy.start()
    for i in range(4):
        feat[i] = features[i][...]
    target = target_ref[...]
    width = held.shape[2]
    total_ref[...] = jnp.zeros_like(total_ref)
    for i in range(4):
        copies[i].wait()
        total = total_ref[...]
        for j in range(width // chunk):
            span = slice(j * chunk, (j + 1) * chunk)
            squared = jnp.dot(target, feat[i, :, span], preferred_element_type=F32)
            panel = jnp.log(squared).astype(BF16)
            total = total + lax.dot_general(
                panel, held[i, :, span], (((1,), (1,)), ((), ())), preferred_element_type=F32
            )
        if i == 3:
            out_ref[...] = (total * (-0.5)).astype(out_ref.dtype)
        else:
            total_ref[...] = total


def sketch_part(target, features, weights, dtype):
    count = target.shape[0]
    width = weights[0].shape[1]
    return pl.pallas_call(
        functools.partial(sketch_kernel, chunk=256),
        out_shape=jax.ShapeDtypeStruct((count, S), dtype),
        in_specs=[vmem()] * 5 + [pl.BlockSpec(memory_space=pl.ANY)] * 4,
        out_specs=vmem(),
        scratch_shapes=[
            pltpu.VMEM((count, S), F32),
            pltpu.VMEM((4, S, width), BF16),
            pltpu.VMEM((4, FEATURES, width), BF16),
            pltpu.SemaphoreType.DMA((4,)),
        ],
        compiler_params=params(),
        name="sketch",
    )(target, *features, *weights)


def swap_cores(value):
    return lax.ppermute(value, "k", [(0, 1), (1, 0)])


def along_z(step, forward):
    pairs = []
    for sz in range(NZ):
        for sk in range(NK):
            other = (sz + (step if sz % 2 else -step)) % NZ
            pair = (sz * NK + sk, other * NK + sk)
            pairs.append(pair if forward else pair[::-1])
    return pairs


def take_rows(pivot_ref, source_ref, out_ref):
    def body(step, carry):
        for i in range(8):
            spot = step * 8 + i
            out_ref[pl.ds(spot, 1), :] = source_ref[pl.ds(pivot_ref[spot], 1), :]
        return carry

    lax.fori_loop(0, K // 8, body, 0)


def sum_kernel(pivot_ref, own_ref, a_ref, b_ref, c_ref, out_ref, chosen_ref):
    others = a_ref[...].astype(F32) + b_ref[...].astype(F32) + c_ref[...].astype(F32)
    out_ref[...] = own_ref[...] + others
    take_rows(pivot_ref, out_ref, chosen_ref)


def choose_kernel(pivot_ref, own_ref, other_ref, chosen_ref, both):
    both[0:K, :] = own_ref[...]
    both[K:, :] = other_ref[...]
    take_rows(pivot_ref, both, chosen_ref)


def choose(pivots, own, other):
    return pl.pallas_call(
        choose_kernel,
        out_shape=jax.ShapeDtypeStruct((K, S), F32),
        in_specs=[smem(), vmem(), vmem()],
        out_specs=vmem(),
        scratch_shapes=[pltpu.VMEM((2 * K, S), F32)],
        compiler_params=params(),
        name="choose",
    )(pivots, own, other)


def eliminate(matrix, i):
    lane = lax.broadcasted_iota(jnp.int32, (1, K), 1)
    line = lax.broadcasted_iota(jnp.int32, (K, 1), 0)
    scale = 1.0 / matrix[i : i + 1, i : i + 1]
    row = (matrix[i : i + 1, :] - jnp.where(lane == i, 1.0, 0.0)) * scale
    column = matrix[:, i : i + 1] - jnp.where(line == i, 1.0, 0.0)
    return matrix - column * row


def dot_rows(left, right):
    return lax.dot_general(
        left,
        right,
        (((1,), (1,)), ((), ())),
        precision=lax.Precision.HIGHEST,
        preferred_element_type=F32,
    )


def tree_kernel(
    pivot_ref, spot_ref, sketch_ref, c0_ref, c1_ref, c2_ref, o2_ref,
    leaf_ref, one_ref, two_ref, three_ref, root_ref,
    both, c3_ref, work,
):
    both[0:K, :] = c2_ref[...]
    both[K:, :] = o2_ref[...]
    take_rows(pivot_ref, both, c3_ref)
    root_ref[...] = c3_ref[pl.ds(pl.multiple_of(spot_ref[2], 16), 16), :]
    lane = lax.broadcasted_iota(jnp.int32, (K, K), 1)
    line = lax.broadcasted_iota(jnp.int32, (K, K), 0)
    eye = lane == line
    chosen = (c0_ref, c1_ref, c2_ref, c3_ref)
    scales = []
    for level, ref in enumerate(chosen):
        rows = ref[...]
        gram = dot_rows(rows, rows)
        trace = jnp.sum(jnp.sum(jnp.where(eye, gram, 0.0), axis=1, keepdims=True), axis=0, keepdims=True)
        scale = 1.0 / (trace / K + 1e-06)
        scales.append(scale)
        work[level] = gram * scale + jnp.where(eye, RIDGE, 0.0)

    def block(step, carry):
        values = [work[level] for level in range(4)]
        for i in range(8):
            values = [eliminate(value, i) for value in values]
        for level in range(4):
            turned = pltpu.roll(values[level], K - 8, 1)
            work[level, 0 : K - 8, :] = turned[8:, :]
            work[level, K - 8 : K, :] = turned[:8, :]
        return carry

    lax.fori_loop(0, K // 8, block, 0)
    shares = (
        sketch_ref[...],
        c0_ref[...],
        c1_ref[pl.ds(pl.multiple_of(spot_ref[0], 64), 64), :],
        c2_ref[pl.ds(pl.multiple_of(spot_ref[1], 32), 32), :],
    )
    outs = (leaf_ref, one_ref, two_ref, three_ref)
    for level in range(4):
        inverse = (jnp.where(eye, 2.0, 0.0) - work[level]) * scales[level]
        right = dot_rows(shares[level], chosen[level][...])
        outs[level][...] = jnp.dot(
            right, inverse, precision=lax.Precision.HIGHEST, preferred_element_type=F32
        )


def body(targets, sources, omega, tree_order, leaf_pivots, pivots_one, pivots_two, pivots_three):
    y, x, z, k = (lax.axis_index(axis) for axis in ALL_AXES)
    leaf = ((y * NX + x) * NZ + z) * NK + k
    bits = (k, z & 1, (z >> 1) & 1)
    tables = (pivots_one, pivots_two, pivots_three)
    pivots = [
        lax.dynamic_index_in_dim(table, leaf >> level + 1, 0, keepdims=False)
        ^ (bits[level] * K).astype(jnp.int32)
        for level, table in enumerate(tables)
    ]

    pad = jnp.zeros((14, sources.shape[1]), BF16)
    block = jnp.concatenate([omega, sources, pad], axis=0)
    far = lax.ppermute(block, "z", [(s, s ^ 1) for s in range(NZ)])
    weights = [block, swap_cores(block), far, swap_cores(far)]
    features = source_features(*weights[:2]) + source_features(*weights[2:])

    own, *others = target_features(targets, tree_order, leaf[None].astype(jnp.int32))
    received = [
        lax.ppermute(sketch_part(others[d - 1], features, weights, BF16), ZK, along_z(d, True))
        for d in (3, 2, 1)
    ]
    mine = sketch_part(own, features, weights, F32)
    sketch, c0 = pl.pallas_call(
        sum_kernel,
        out_shape=[jax.ShapeDtypeStruct((LEAF, S), F32), jax.ShapeDtypeStruct((K, S), F32)],
        in_specs=[smem()] + [vmem()] * 4,
        out_specs=[vmem()] * 2,
        compiler_params=params(),
        name="sum",
    )(leaf_pivots[0], mine, *received)
    c1 = choose(pivots[0], c0, swap_cores(c0))
    c2 = choose(pivots[1], c1, lax.ppermute(c1, "z", [(s, s ^ 1) for s in range(NZ)]))
    other2 = lax.ppermute(c2, "z", [(s, s ^ 2) for s in range(NZ)])
    spots = jnp.stack(
        [k * 64, ((z & 1) * 2 + k) * 32, ((z & 3) * 2 + k) * 16]
    ).astype(jnp.int32)
    return pl.pallas_call(
        tree_kernel,
        out_shape=[
            jax.ShapeDtypeStruct((LEAF, K), F32),
            jax.ShapeDtypeStruct((K, K), F32),
            jax.ShapeDtypeStruct((K // 2, K), F32),
            jax.ShapeDtypeStruct((K // 4, K), F32),
            jax.ShapeDtypeStruct((K // 8, S), F32),
        ],
        in_specs=[smem()] * 2 + [vmem()] * 5,
        out_specs=[vmem()] * 5,
        scratch_shapes=[
            pltpu.VMEM((2 * K, S), F32),
            pltpu.VMEM((K, S), F32),
            pltpu.VMEM((4, K, K), F32),
        ],
        compiler_params=params(),
        name="tree",
    )(pivots[2], spots, sketch, c0, c1, c2, other2)


def solution(mesh):
    finer = Mesh(mesh.devices.reshape(NY, NX, NZ, NK), ALL_AXES)
    col = ("z", "k")
    placed = (
        P(None, ALL_AXES),
        P(None, col),
        P(None, col),
        P(ALL_AXES),
        P(ALL_AXES, None),
        P(),
        P(),
        P(),
    )
    return jax.shard_map(
        body,
        mesh=finer,
        in_specs=placed,
        out_specs=(P(ALL_AXES, None),) * 5,
        check_vma=False,
    )
```

```python
import functools

import jax
import jax.numpy as jnp
from jax import lax
from jax.experimental import pallas as pl
from jax.experimental.pallas import tpu as pltpu
from jax.sharding import Mesh
from jax.sharding import PartitionSpec as P

LEAF = 512
S = 256
K = 128
FEATURES = 16
RIDGE = 0.1
DELTA_SQUARED = 0.0001
ALL_AXES = ("y", "x", "z", "k")
ZK = ("z", "k")
NY, NX, NZ, NK = 4, 4, 8, 2
F32 = jnp.float32
BF16 = jnp.bfloat16
VMEM_LIMIT = 40 << 20


def params():
    return pltpu.CompilerParams(vmem_limit_bytes=VMEM_LIMIT)


def smem():
    return pl.BlockSpec(memory_space=pltpu.SMEM)


def vmem():
    return pl.BlockSpec(memory_space=pltpu.VMEM)


def split3(value):
    high = value.astype(BF16).astype(F32)
    rest = value - high
    middle = rest.astype(BF16).astype(F32)
    low = (rest - middle).astype(BF16).astype(F32)
    return high, middle, low


def lookup_kernel(me_ref, own_ref, other_ref, *refs):
    lists, outs, (thirds,) = refs[:4], refs[4:8], refs[8:]
    for side, table_ref in enumerate((own_ref, other_ref)):
        for coord in range(2):
            values = table_ref[pl.ds(coord, LEAF, stride=2), :]
            for third, part in enumerate(split3(values)):
                thirds[third, side * LEAF : (side + 1) * LEAF, coord * 128 : coord * 128 + 128] = (
                    part.astype(BF16)
                )
    core = me_ref[0]
    line = lax.broadcasted_iota(jnp.int32, (LEAF, 1024), 1)
    lane = lax.broadcasted_iota(jnp.int32, (LEAF, 128), 1)
    slot = lax.broadcasted_iota(jnp.int32, (LEAF, FEATURES), 1)
    for index_ref, out_ref in zip(lists, outs):
        order = jnp.broadcast_to(index_ref[...].astype(F32), (8, LEAF))
        index = jnp.transpose(order)[:, 0:1].astype(jnp.int32)
        row = (((index >> 9) & 1) ^ core) * LEAF + (index >> 10) * 4 + ((index >> 7) & 3)
        hot = jnp.where(line == row, 1.0, 0.0).astype(BF16)
        rows = jnp.dot(hot, thirds[0], preferred_element_type=F32)
        for third in (1, 2):
            rows = rows + jnp.dot(hot, thirds[third], preferred_element_type=F32)
        mask = lane == (index & 127)
        tx = jnp.sum(jnp.where(mask, rows[:, :128], 0.0), axis=1, keepdims=True)
        ty = jnp.sum(jnp.where(mask, rows[:, 128:], 0.0), axis=1, keepdims=True)
        columns = list(split3(tx)) + list(split3(ty))
        columns += list(split3(tx * tx + (ty * ty + DELTA_SQUARED)))
        feature = jnp.where(slot < 12, 1.0, 0.0)
        for i, column in enumerate(columns):
            feature = jnp.where(slot == i, column, feature)
        out_ref[...] = feature.astype(BF16)


def copies_from(value, axis, size):
    copies = jnp.broadcast_to(value[None], (size, *value.shape))
    parts = lax.all_to_all(copies, axis, split_axis=0, concat_axis=0, tiled=True)
    return parts.reshape(size * value.shape[0], *value.shape[1:])


def target_tables(targets, lists):
    own = targets.reshape(2, 4, 128).transpose(1, 0, 2).reshape(8, 128)
    table = copies_from(own, "z", NZ)
    table, *lists = lax.optimization_barrier((table, *lists))
    table = copies_from(table, ("y", "x"), NY * NX)
    return (table, swap_cores(table), *lists)


def target_features(tables, core):
    return pl.pallas_call(
        lookup_kernel,
        out_shape=[jax.ShapeDtypeStruct((LEAF, FEATURES), BF16)] * 4,
        in_specs=[smem()] + [vmem()] * 6,
        out_specs=[vmem()] * 4,
        scratch_shapes=[pltpu.VMEM((3, 1024, 256), BF16)],
        compiler_params=params(),
        name="lookup",
    )(core, *tables)


def source_kernel(*refs):
    half = len(refs) // 2
    for source_ref, out_ref in zip(refs[:half], refs[half:]):
        points = source_ref[...].astype(F32)
        sx, sy = points[0:1], points[1:2]
        size = split3(sx * sx + sy * sy)
        one = jnp.ones_like(sx)
        zero = jnp.zeros_like(sx)
        rows = [-2.0 * sx] * 3 + [-2.0 * sy] * 3 + list(size) + [zero] * 4
        rows = rows[:6] + [one] * 3 + rows[6:]
        out_ref[...] = jnp.concatenate(rows, axis=0).astype(BF16)


def source_features(*blocks):
    width = blocks[0].shape[1]
    return pl.pallas_call(
        source_kernel,
        grid=(1,),
        out_shape=[jax.ShapeDtypeStruct((FEATURES, width), BF16)] * len(blocks),
        in_specs=[pl.BlockSpec((16, width), lambda i: (S // 16, 0))] * len(blocks),
        out_specs=[pl.BlockSpec((FEATURES, width), lambda i: (0, 0))] * len(blocks),
        compiler_params=params(),
        name="source_features",
    )(*blocks)


def sketch_kernel(target_ref, *refs, chunk):
    features, weights, (out_ref, total_ref, held, feat, sems) = refs[:4], refs[4:8], refs[8:]
    copies = [
        pltpu.make_async_copy(weight.at[pl.ds(0, S)], held.at[i], sems.at[i])
        for i, weight in enumerate(weights)
    ]
    for copy in copies:
        copy.start()
    for i in range(4):
        feat[i] = features[i][...]
    target = target_ref[...]
    width = held.shape[2]
    total_ref[...] = jnp.zeros_like(total_ref)
    for i in range(4):
        copies[i].wait()
        total = total_ref[...]
        for j in range(width // chunk):
            span = slice(j * chunk, (j + 1) * chunk)
            squared = jnp.dot(target, feat[i, :, span], preferred_element_type=F32)
            panel = jnp.log(squared).astype(BF16)
            total = total + lax.dot_general(
                panel, held[i, :, span], (((1,), (1,)), ((), ())), preferred_element_type=F32
            )
        if i == 3:
            out_ref[...] = (total * (-0.5)).astype(out_ref.dtype)
        else:
            total_ref[...] = total


def sketch_part(target, features, weights, dtype):
    count = target.shape[0]
    width = weights[0].shape[1]
    return pl.pallas_call(
        functools.partial(sketch_kernel, chunk=256),
        out_shape=jax.ShapeDtypeStruct((count, S), dtype),
        in_specs=[vmem()] * 5 + [pl.BlockSpec(memory_space=pl.ANY)] * 4,
        out_specs=vmem(),
        scratch_shapes=[
            pltpu.VMEM((count, S), F32),
            pltpu.VMEM((4, S, width), BF16),
            pltpu.VMEM((4, FEATURES, width), BF16),
            pltpu.SemaphoreType.DMA((4,)),
        ],
        compiler_params=params(),
        name="sketch",
    )(target, *features, *weights)


def swap_cores(value):
    return lax.ppermute(value, "k", [(0, 1), (1, 0)])


def along_z(step, forward):
    pairs = []
    for sz in range(NZ):
        for sk in range(NK):
            other = (sz + (step if sz % 2 else -step)) % NZ
            pair = (sz * NK + sk, other * NK + sk)
            pairs.append(pair if forward else pair[::-1])
    return pairs


def take_rows(pivot_ref, source_ref, out_ref):
    def body(step, carry):
        for i in range(8):
            spot = step * 8 + i
            out_ref[pl.ds(spot, 1), :] = source_ref[pl.ds(pivot_ref[spot], 1), :]
        return carry

    lax.fori_loop(0, K // 8, body, 0)


def sum_kernel(pivot_ref, own_ref, a_ref, b_ref, c_ref, out_ref, chosen_ref):
    others = a_ref[...].astype(F32) + b_ref[...].astype(F32) + c_ref[...].astype(F32)
    out_ref[...] = own_ref[...] + others
    take_rows(pivot_ref, out_ref, chosen_ref)


def choose_kernel(pivot_ref, own_ref, other_ref, chosen_ref, both):
    both[0:K, :] = own_ref[...]
    both[K:, :] = other_ref[...]
    take_rows(pivot_ref, both, chosen_ref)


def choose(pivots, own, other):
    return pl.pallas_call(
        choose_kernel,
        out_shape=jax.ShapeDtypeStruct((K, S), F32),
        in_specs=[smem(), vmem(), vmem()],
        out_specs=vmem(),
        scratch_shapes=[pltpu.VMEM((2 * K, S), F32)],
        compiler_params=params(),
        name="choose",
    )(pivots, own, other)


def eliminate(matrix, i):
    lane = lax.broadcasted_iota(jnp.int32, (1, K), 1)
    line = lax.broadcasted_iota(jnp.int32, (K, 1), 0)
    scale = 1.0 / matrix[i : i + 1, i : i + 1]
    row = (matrix[i : i + 1, :] - jnp.where(lane == i, 1.0, 0.0)) * scale
    column = matrix[:, i : i + 1] - jnp.where(line == i, 1.0, 0.0)
    return matrix - column * row


def dot_rows(left, right):
    return lax.dot_general(
        left,
        right,
        (((1,), (1,)), ((), ())),
        precision=lax.Precision.HIGHEST,
        preferred_element_type=F32,
    )


def tree_kernel(
    pivot_ref, spot_ref, sketch_ref, c0_ref, c1_ref, c2_ref, o2_ref,
    leaf_ref, one_ref, two_ref, three_ref, root_ref,
    both, c3_ref, work,
):
    both[0:K, :] = c2_ref[...]
    both[K:, :] = o2_ref[...]
    take_rows(pivot_ref, both, c3_ref)
    root_ref[...] = c3_ref[pl.ds(pl.multiple_of(spot_ref[2], 16), 16), :]
    lane = lax.broadcasted_iota(jnp.int32, (K, K), 1)
    line = lax.broadcasted_iota(jnp.int32, (K, K), 0)
    eye = lane == line
    chosen = (c0_ref, c1_ref, c2_ref, c3_ref)
    scales = []
    for level, ref in enumerate(chosen):
        rows = ref[...]
        gram = dot_rows(rows, rows)
        trace = jnp.sum(jnp.sum(jnp.where(eye, gram, 0.0), axis=1, keepdims=True), axis=0, keepdims=True)
        scale = 1.0 / (trace / K + 1e-06)
        scales.append(scale)
        work[level] = gram * scale + jnp.where(eye, RIDGE, 0.0)

    def block(step, carry):
        values = [work[level] for level in range(4)]
        for i in range(8):
            values = [eliminate(value, i) for value in values]
        for level in range(4):
            turned = pltpu.roll(values[level], K - 8, 1)
            work[level, 0 : K - 8, :] = turned[8:, :]
            work[level, K - 8 : K, :] = turned[:8, :]
        return carry

    lax.fori_loop(0, K // 8, block, 0)
    shares = (
        sketch_ref[...],
        c0_ref[...],
        c1_ref[pl.ds(pl.multiple_of(spot_ref[0], 64), 64), :],
        c2_ref[pl.ds(pl.multiple_of(spot_ref[1], 32), 32), :],
    )
    outs = (leaf_ref, one_ref, two_ref, three_ref)
    for level in range(4):
        inverse = (jnp.where(eye, 2.0, 0.0) - work[level]) * scales[level]
        right = dot_rows(shares[level], chosen[level][...])
        outs[level][...] = jnp.dot(
            right, inverse, precision=lax.Precision.HIGHEST, preferred_element_type=F32
        )


def body(targets, sources, omega, tree_order, leaf_pivots, pivots_one, pivots_two, pivots_three):
    y, x, z, k = (lax.axis_index(axis) for axis in ALL_AXES)
    leaf = ((y * NX + x) * NZ + z) * NK + k
    bits = (k, z & 1, (z >> 1) & 1)
    tables = (pivots_one, pivots_two, pivots_three)
    pivots = [
        lax.dynamic_index_in_dim(table, leaf >> level + 1, 0, keepdims=False)
        ^ (bits[level] * K).astype(jnp.int32)
        for level, table in enumerate(tables)
    ]

    order = tree_order.reshape(1, LEAF)
    lists = [order] + [lax.ppermute(order, ZK, along_z(d, False)) for d in (1, 2, 3)]
    pad = jnp.zeros((14, sources.shape[1]), BF16)
    block = jnp.concatenate([omega, sources, pad], axis=0)
    far = lax.ppermute(block, "z", [(s, s ^ 1) for s in range(NZ)])
    weights = [block, swap_cores(block)]
    features = source_features(*weights)
    tables = target_tables(targets, lists)
    far, pivots, tables = lax.optimization_barrier((far, pivots, tables))
    weights += [far, swap_cores(far)]
    features += source_features(*weights[2:])
    own, *others = target_features(tables, k[None].astype(jnp.int32))
    received = [
        lax.ppermute(sketch_part(others[d - 1], features, weights, BF16), ZK, along_z(d, True))
        for d in (3, 2, 1)
    ]
    mine = sketch_part(own, features, weights, F32)
    sketch, c0 = pl.pallas_call(
        sum_kernel,
        out_shape=[jax.ShapeDtypeStruct((LEAF, S), F32), jax.ShapeDtypeStruct((K, S), F32)],
        in_specs=[smem()] + [vmem()] * 4,
        out_specs=[vmem()] * 2,
        compiler_params=params(),
        name="sum",
    )(leaf_pivots[0], mine, *received)
    c1 = choose(pivots[0], c0, swap_cores(c0))
    c2 = choose(pivots[1], c1, lax.ppermute(c1, "z", [(s, s ^ 1) for s in range(NZ)]))
    other2 = lax.ppermute(c2, "z", [(s, s ^ 2) for s in range(NZ)])
    spots = jnp.stack(
        [k * 64, ((z & 1) * 2 + k) * 32, ((z & 3) * 2 + k) * 16]
    ).astype(jnp.int32)
    return pl.pallas_call(
        tree_kernel,
        out_shape=[
            jax.ShapeDtypeStruct((LEAF, K), F32),
            jax.ShapeDtypeStruct((K, K), F32),
            jax.ShapeDtypeStruct((K // 2, K), F32),
            jax.ShapeDtypeStruct((K // 4, K), F32),
            jax.ShapeDtypeStruct((K // 8, S), F32),
        ],
        in_specs=[smem()] * 2 + [vmem()] * 5,
        out_specs=[vmem()] * 5,
        scratch_shapes=[
            pltpu.VMEM((2 * K, S), F32),
            pltpu.VMEM((K, S), F32),
            pltpu.VMEM((4, K, K), F32),
        ],
        compiler_params=params(),
        name="tree",
    )(pivots[2], spots, sketch, c0, c1, c2, other2)


def solution(mesh):
    finer = Mesh(mesh.devices.reshape(NY, NX, NZ, NK), ALL_AXES)
    col = ("z", "k")
    placed = (
        P(None, ALL_AXES),
        P(None, col),
        P(None, col),
        P(ALL_AXES),
        P(ALL_AXES, None),
        P(),
        P(),
        P(),
    )
    return jax.shard_map(
        body,
        mesh=finer,
        in_specs=placed,
        out_specs=(P(ALL_AXES, None),) * 5,
        check_vma=False,
    )
```

```python
import functools

import jax
import jax.numpy as jnp
from jax import lax
from jax.experimental import pallas as pl
from jax.experimental.pallas import tpu as pltpu
from jax.sharding import Mesh
from jax.sharding import PartitionSpec as P

LEAF = 512
S = 256
K = 128
FEATURES = 16
BLOCK = 16
RIDGE = 0.1
DELTA_SQUARED = 0.0001
ALL_AXES = ("y", "x", "z", "k")
ZK = ("z", "k")
NY, NX, NZ, NK = 4, 4, 8, 2
F32 = jnp.float32
BF16 = jnp.bfloat16
VMEM_LIMIT = 40 << 20


def params():
    return pltpu.CompilerParams(vmem_limit_bytes=VMEM_LIMIT)


def smem():
    return pl.BlockSpec(memory_space=pltpu.SMEM)


def vmem():
    return pl.BlockSpec(memory_space=pltpu.VMEM)


def split3(value):
    high = value.astype(BF16).astype(F32)
    rest = value - high
    middle = rest.astype(BF16).astype(F32)
    low = (rest - middle).astype(BF16).astype(F32)
    return high, middle, low


def lookup_kernel(me_ref, own_ref, other_ref, *refs):
    lists, outs, (halves,) = refs[:4], refs[4:8], refs[8:]
    for side, table_ref in enumerate((own_ref, other_ref)):
        for coord in range(2):
            values = table_ref[pl.ds(coord, LEAF, stride=2), :]
            for half, part in enumerate(split3(values)[:2]):
                halves[half, side * LEAF : (side + 1) * LEAF, coord * 128 : coord * 128 + 128] = (
                    part.astype(BF16)
                )
    core = me_ref[0]
    line = lax.broadcasted_iota(jnp.int32, (LEAF, 1024), 1)
    lane = lax.broadcasted_iota(jnp.int32, (LEAF, 128), 1)
    slot = lax.broadcasted_iota(jnp.int32, (LEAF, FEATURES), 1)
    for index_ref, out_ref in zip(lists, outs):
        order = jnp.broadcast_to(index_ref[...].astype(F32), (8, LEAF))
        index = jnp.transpose(order)[:, 0:1].astype(jnp.int32)
        row = (((index >> 9) & 1) ^ core) * LEAF + (index >> 10) * 4 + ((index >> 7) & 3)
        hot = jnp.where(line == row, 1.0, 0.0).astype(BF16)
        rows = jnp.dot(hot, halves[0], preferred_element_type=F32)
        rows = rows + jnp.dot(hot, halves[1], preferred_element_type=F32)
        mask = lane == (index & 127)
        tx = jnp.sum(jnp.where(mask, rows[:, :128], 0.0), axis=1, keepdims=True)
        ty = jnp.sum(jnp.where(mask, rows[:, 128:], 0.0), axis=1, keepdims=True)
        columns = list(split3(tx)[:2]) + list(split3(ty)[:2])
        columns += list(split3(tx * tx + (ty * ty + DELTA_SQUARED)))
        feature = jnp.where(slot < 10, 1.0, 0.0)
        for i, column in enumerate(columns):
            feature = jnp.where(slot == i, column, feature)
        out_ref[...] = feature.astype(BF16)


def copies_from(value, axis, size):
    copies = jnp.broadcast_to(value[None], (size, *value.shape))
    parts = lax.all_to_all(copies, axis, split_axis=0, concat_axis=0, tiled=True)
    return parts.reshape(size * value.shape[0], *value.shape[1:])


def target_features(tables, core):
    return pl.pallas_call(
        lookup_kernel,
        out_shape=[jax.ShapeDtypeStruct((LEAF, FEATURES), BF16)] * 4,
        in_specs=[smem()] + [vmem()] * 6,
        out_specs=[vmem()] * 4,
        scratch_shapes=[pltpu.VMEM((2, 1024, 256), BF16)],
        compiler_params=params(),
        name="lookup",
    )(core, *tables)


def source_kernel(*refs):
    half = len(refs) // 2
    for source_ref, out_ref in zip(refs[:half], refs[half:]):
        points = source_ref[...].astype(F32)
        sx, sy = points[0:1], points[1:2]
        size = split3(sx * sx + sy * sy)
        one = jnp.ones_like(sx)
        zero = jnp.zeros_like(sx)
        rows = [-2.0 * sx] * 2 + [-2.0 * sy] * 2 + [one] * 3 + list(size) + [zero] * 6
        out_ref[...] = jnp.concatenate(rows, axis=0).astype(BF16)


def source_features(*blocks):
    width = blocks[0].shape[1]
    return pl.pallas_call(
        source_kernel,
        grid=(1,),
        out_shape=[jax.ShapeDtypeStruct((FEATURES, width), BF16)] * len(blocks),
        in_specs=[pl.BlockSpec((16, width), lambda i: (S // 16, 0))] * len(blocks),
        out_specs=[pl.BlockSpec((FEATURES, width), lambda i: (0, 0))] * len(blocks),
        compiler_params=params(),
        name="source_features",
    )(*blocks)


def sketch_kernel(target_ref, *refs, chunk):
    features, weights, (out_ref, total_ref, held, feat, sems) = refs[:4], refs[4:8], refs[8:]
    copies = [
        pltpu.make_async_copy(weight.at[pl.ds(0, S)], held.at[i], sems.at[i])
        for i, weight in enumerate(weights)
    ]
    for copy in copies:
        copy.start()
    for i in range(4):
        feat[i] = features[i][...]
    target = target_ref[...]
    width = held.shape[2]
    total_ref[...] = jnp.zeros_like(total_ref)
    for i in range(4):
        copies[i].wait()
        total = total_ref[...]
        for j in range(width // chunk):
            span = slice(j * chunk, (j + 1) * chunk)
            squared = jnp.dot(target, feat[i, :, span], preferred_element_type=F32)
            panel = jnp.log(squared).astype(BF16)
            total = total + lax.dot_general(
                panel, held[i, :, span], (((1,), (1,)), ((), ())), preferred_element_type=F32
            )
        if i == 3:
            out_ref[...] = (total * (-0.5)).astype(out_ref.dtype)
        else:
            total_ref[...] = total


def sketch_part(target, features, weights, dtype):
    count = target.shape[0]
    width = weights[0].shape[1]
    return pl.pallas_call(
        functools.partial(sketch_kernel, chunk=256),
        out_shape=jax.ShapeDtypeStruct((count, S), dtype),
        in_specs=[vmem()] * 5 + [pl.BlockSpec(memory_space=pl.ANY)] * 4,
        out_specs=vmem(),
        scratch_shapes=[
            pltpu.VMEM((count, S), F32),
            pltpu.VMEM((4, S, width), BF16),
            pltpu.VMEM((4, FEATURES, width), BF16),
            pltpu.SemaphoreType.DMA((4,)),
        ],
        compiler_params=params(),
        name="sketch",
    )(target, *features, *weights)


def swap_cores(value):
    return lax.ppermute(value, "k", [(0, 1), (1, 0)])


def along_z(step, forward):
    pairs = []
    for sz in range(NZ):
        for sk in range(NK):
            other = (sz + (step if sz % 2 else -step)) % NZ
            pair = (sz * NK + sk, other * NK + sk)
            pairs.append(pair if forward else pair[::-1])
    return pairs


def take_rows(pivot_ref, source_ref, out_ref):
    def body(step, carry):
        for i in range(8):
            spot = step * 8 + i
            out_ref[pl.ds(spot, 1), :] = source_ref[pl.ds(pivot_ref[spot], 1), :]
        return carry

    lax.fori_loop(0, K // 8, body, 0)


def sum_kernel(pivot_ref, own_ref, a_ref, b_ref, c_ref, out_ref, chosen_ref):
    others = a_ref[...].astype(F32) + b_ref[...].astype(F32) + c_ref[...].astype(F32)
    out_ref[...] = own_ref[...] + others
    take_rows(pivot_ref, out_ref, chosen_ref)


def choose_kernel(pivot_ref, own_ref, other_ref, chosen_ref, both):
    both[0:K, :] = own_ref[...]
    both[K:, :] = other_ref[...]
    take_rows(pivot_ref, both, chosen_ref)


def choose(pivots, own, other):
    return pl.pallas_call(
        choose_kernel,
        out_shape=jax.ShapeDtypeStruct((K, S), F32),
        in_specs=[smem(), vmem(), vmem()],
        out_specs=vmem(),
        scratch_shapes=[pltpu.VMEM((2 * K, S), F32)],
        compiler_params=params(),
        name="choose",
    )(pivots, own, other)


def eliminate(matrix, i):
    lane = lax.broadcasted_iota(jnp.int32, (1, K), 1)
    line = lax.broadcasted_iota(jnp.int32, (K, K), 0)
    columns = [jnp.broadcast_to(matrix[:, i + t : i + t + 1], (K, K)) for t in range(4)]
    pivot = [[columns[u][i + t : i + t + 1, :] for u in range(4)] for t in range(4)]
    rows = [matrix[i + t : i + t + 1, :] - jnp.where(lane == i + t, 1.0, 0.0) for t in range(4)]

    def inverse(m):
        (p, q), (r, s) = m
        scale = 1.0 / (p * s - q * r)
        return [[s * scale, -q * scale], [-r * scale, p * scale]]

    def product(m, v):
        return [m[t][0] * v[0] + m[t][1] * v[1] for t in range(2)]

    a, b = [row[:2] for row in pivot[:2]], [row[2:] for row in pivot[:2]]
    c, d = [row[:2] for row in pivot[2:]], [row[2:] for row in pivot[2:]]
    upper = inverse(a)
    mixed = [[c[t][0] * upper[0][u] + c[t][1] * upper[1][u] for u in range(2)] for t in range(2)]
    rest = [
        [d[t][u] - (mixed[t][0] * b[0][u] + mixed[t][1] * b[1][u]) for u in range(2)]
        for t in range(2)
    ]
    step = product(mixed, rows[:2])
    last = product(inverse(rest), [rows[2] - step[0], rows[3] - step[1]])
    step = product(b, last)
    first = product(upper, [rows[0] - step[0], rows[1] - step[1]])
    for t, row in enumerate(first + last):
        matrix = matrix - (columns[t] - jnp.where(line == i + t, 1.0, 0.0)) * row
    return matrix


def dot_rows(left, right):
    return lax.dot_general(
        left,
        right,
        (((1,), (1,)), ((), ())),
        precision=lax.Precision.HIGHEST,
        preferred_element_type=F32,
    )


def interpolate(chosen, shares, outs, work):
    lane = lax.broadcasted_iota(jnp.int32, (K, K), 1)
    line = lax.broadcasted_iota(jnp.int32, (K, K), 0)
    eye = lane == line
    count = len(chosen)
    scales = []
    for level, rows in enumerate(chosen):
        gram = dot_rows(rows, rows)
        trace = jnp.sum(jnp.where(eye, gram, 0.0), axis=1, keepdims=True)
        trace = jnp.sum(trace, axis=0, keepdims=True)
        scale = 1.0 / (trace / K + 1e-06)
        scales.append(scale)
        work[level] = gram * scale + jnp.where(eye, RIDGE, 0.0)

    def block(step, carry):
        values = [work[level] for level in range(count)]
        for i in range(0, BLOCK, 4):
            values = [eliminate(value, i) for value in values]
        for level in range(count):
            turned = pltpu.roll(values[level], K - BLOCK, 1)
            work[level, 0 : K - BLOCK, :] = turned[BLOCK:, :]
            work[level, K - BLOCK : K, :] = turned[:BLOCK, :]
        return carry

    lax.fori_loop(0, K // BLOCK, block, 0)
    for level in range(count):
        inverse = (jnp.where(eye, 2.0, 0.0) - work[level]) * scales[level]
        right = dot_rows(shares[level], chosen[level])
        outs[level][...] = jnp.dot(
            right, inverse, precision=lax.Precision.HIGHEST, preferred_element_type=F32
        )


def leaf_kernel(sketch_ref, c0_ref, out_ref, work):
    interpolate([c0_ref[...]], [sketch_ref[...]], [out_ref], work)


def middle_kernel(spot_ref, c0_ref, c1_ref, c2_ref, one_ref, two_ref, work):
    share = c1_ref[pl.ds(pl.multiple_of(spot_ref[0], 64), 64), :]
    interpolate(
        [c1_ref[...], c2_ref[...]], [c0_ref[...], share], [one_ref, two_ref], work
    )


def top_kernel(pivot_ref, spot_ref, c2_ref, o2_ref, three_ref, root_ref, both, c3_ref, work):
    both[0:K, :] = c2_ref[...]
    both[K:, :] = o2_ref[...]
    take_rows(pivot_ref, both, c3_ref)
    root_ref[...] = c3_ref[pl.ds(pl.multiple_of(spot_ref[2], 16), 16), :]
    share = c2_ref[pl.ds(pl.multiple_of(spot_ref[1], 32), 32), :]
    interpolate([c3_ref[...]], [share], [three_ref], work)


def body(targets, sources, omega, tree_order, leaf_pivots, pivots_one, pivots_two, pivots_three):
    y, x, z, k = (lax.axis_index(axis) for axis in ALL_AXES)
    leaf = ((y * NX + x) * NZ + z) * NK + k
    bits = (k, z & 1, (z >> 1) & 1)
    tables = (pivots_one, pivots_two, pivots_three)
    pivots = [
        lax.dynamic_index_in_dim(table, leaf >> level + 1, 0, keepdims=False)
        ^ (bits[level] * K).astype(jnp.int32)
        for level, table in enumerate(tables)
    ]

    spots = jnp.stack([k * 64, ((z & 1) * 2 + k) * 32, ((z & 3) * 2 + k) * 16]).astype(jnp.int32)
    order = tree_order.reshape(1, LEAF)
    lists = [order] + [lax.ppermute(order, ZK, along_z(d, False)) for d in (1, 2, 3)]
    table = targets.reshape(2, 4, 128).transpose(1, 0, 2).reshape(8, 128)
    table = copies_from(table, "z", NZ)
    pad = jnp.zeros((14, sources.shape[1]), BF16)
    block = jnp.concatenate([omega, sources, pad], axis=0)
    table, lists, block = lax.optimization_barrier((table, lists, block))
    far = lax.ppermute(block, "z", [(s, s ^ 1) for s in range(NZ)])
    weights = [block, swap_cores(block)]
    features = source_features(*weights)
    table = copies_from(table, ("y", "x"), NY * NX)
    tables = [table, swap_cores(table), *lists]
    pivots, spots, tables = lax.optimization_barrier((pivots, spots, tables))
    own, *others = target_features(tables, k[None].astype(jnp.int32))
    far, own, others = lax.optimization_barrier((far, own, others))
    weights += [far, swap_cores(far)]
    features += source_features(*weights[2:])
    received = [
        lax.ppermute(sketch_part(others[d - 1], features, weights, BF16), ZK, along_z(d, True))
        for d in (3, 2, 1)
    ]
    mine = sketch_part(own, features, weights, F32)
    sketch, c0 = pl.pallas_call(
        sum_kernel,
        out_shape=[jax.ShapeDtypeStruct((LEAF, S), F32), jax.ShapeDtypeStruct((K, S), F32)],
        in_specs=[smem()] + [vmem()] * 4,
        out_specs=[vmem()] * 2,
        compiler_params=params(),
        name="sum",
    )(leaf_pivots[0], mine, *received)
    c1 = choose(pivots[0], c0, swap_cores(c0))
    other1 = lax.ppermute(c1, "z", [(s, s ^ 1) for s in range(NZ)])
    sketch, c0, c1 = lax.optimization_barrier((sketch, c0, c1))
    leaf_out = pl.pallas_call(
        leaf_kernel,
        out_shape=jax.ShapeDtypeStruct((LEAF, K), F32),
        in_specs=[vmem()] * 2,
        out_specs=vmem(),
        scratch_shapes=[pltpu.VMEM((1, K, K), F32)],
        compiler_params=params(),
        name="leaf_interp",
    )(sketch, c0)
    other1, leaf_out = lax.optimization_barrier((other1, leaf_out))
    c2 = choose(pivots[1], c1, other1)
    other2 = lax.ppermute(c2, "z", [(s, s ^ 2) for s in range(NZ)])
    one_out, two_out = pl.pallas_call(
        middle_kernel,
        out_shape=[jax.ShapeDtypeStruct((K, K), F32), jax.ShapeDtypeStruct((K // 2, K), F32)],
        in_specs=[smem()] + [vmem()] * 3,
        out_specs=[vmem()] * 2,
        scratch_shapes=[pltpu.VMEM((2, K, K), F32)],
        compiler_params=params(),
        name="middle_interp",
    )(spots, c0, c1, c2)
    three_out, root = pl.pallas_call(
        top_kernel,
        out_shape=[jax.ShapeDtypeStruct((K // 4, K), F32), jax.ShapeDtypeStruct((K // 8, S), F32)],
        in_specs=[smem()] * 2 + [vmem()] * 2,
        out_specs=[vmem()] * 2,
        scratch_shapes=[
            pltpu.VMEM((2 * K, S), F32),
            pltpu.VMEM((K, S), F32),
            pltpu.VMEM((1, K, K), F32),
        ],
        compiler_params=params(),
        name="top_interp",
    )(pivots[2], spots, c2, other2)
    return leaf_out, one_out, two_out, three_out, root


def solution(mesh):
    finer = Mesh(mesh.devices.reshape(NY, NX, NZ, NK), ALL_AXES)
    col = ("z", "k")
    placed = (
        P(None, ALL_AXES),
        P(None, col),
        P(None, col),
        P(ALL_AXES),
        P(ALL_AXES, None),
        P(),
        P(),
        P(),
    )
    return jax.shard_map(
        body,
        mesh=finer,
        in_specs=placed,
        out_specs=(P(ALL_AXES, None),) * 5,
        check_vma=False,
    )
```

```python
import functools

import jax
import jax.numpy as jnp
from jax import lax
from jax.experimental import pallas as pl
from jax.experimental.pallas import tpu as pltpu
from jax.sharding import Mesh
from jax.sharding import PartitionSpec as P

LEAF = 512
S = 256
K = 128
FEATURES = 16
BLOCK = 16
PIVOT = 2
RIDGE = 0.1
DELTA_SQUARED = 0.0001
ALL_AXES = ("y", "x", "z", "k")
ZK = ("z", "k")
NY, NX, NZ, NK = 4, 4, 8, 2
F32 = jnp.float32
BF16 = jnp.bfloat16
VMEM_LIMIT = 40 << 20


def params():
    return pltpu.CompilerParams(vmem_limit_bytes=VMEM_LIMIT)


def smem():
    return pl.BlockSpec(memory_space=pltpu.SMEM)


def vmem():
    return pl.BlockSpec(memory_space=pltpu.VMEM)


def split3(value):
    high = value.astype(BF16).astype(F32)
    rest = value - high
    middle = rest.astype(BF16).astype(F32)
    low = (rest - middle).astype(BF16).astype(F32)
    return high, middle, low


def lookup_kernel(me_ref, own_ref, other_ref, note_ref, *refs):
    outs, chosen_ref, halves = refs[:4], refs[4], refs[5]
    for side, table_ref in enumerate((own_ref, other_ref)):
        for coord in range(2):
            values = table_ref[pl.ds(coord, LEAF, stride=2), :]
            for half, part in enumerate(split3(values)[:2]):
                halves[half, side * LEAF : (side + 1) * LEAF, coord * 128 : coord * 128 + 128] = (
                    part.astype(BF16)
                )
    core = me_ref[0]
    line = lax.broadcasted_iota(jnp.int32, (LEAF, 1024), 1)
    spot = lax.broadcasted_iota(jnp.int32, (K, LEAF), 1)
    lane = lax.broadcasted_iota(jnp.int32, (LEAF, 128), 1)
    slot = lax.broadcasted_iota(jnp.int32, (LEAF, FEATURES), 1)
    for leaf, out_ref in enumerate(outs):
        note = jnp.transpose(note_ref[me_ref[1 + leaf]])
        index = jnp.concatenate([note[:, i : i + 1] for i in range(4)], axis=0).astype(jnp.int32)
        row = (((index >> 9) & 1) ^ core) * LEAF + (index >> 10) * 4 + ((index >> 7) & 3)
        hot = jnp.where(line == row, 1.0, 0.0).astype(BF16)
        rows = jnp.dot(hot, halves[0], preferred_element_type=F32)
        rows = rows + jnp.dot(hot, halves[1], preferred_element_type=F32)
        mask = lane == (index & 127)
        tx = jnp.sum(jnp.where(mask, rows[:, :128], 0.0), axis=1, keepdims=True)
        ty = jnp.sum(jnp.where(mask, rows[:, 128:], 0.0), axis=1, keepdims=True)
        columns = list(split3(tx)[:2]) + list(split3(ty)[:2])
        columns += list(split3(tx * tx + (ty * ty + DELTA_SQUARED)))
        feature = jnp.where(slot < 10, 1.0, 0.0)
        for i, column in enumerate(columns):
            feature = jnp.where(slot == i, column, feature)
        feature = feature.astype(BF16)
        out_ref[...] = feature
        picked = jnp.where(spot == note[:, 4:5].astype(jnp.int32), 1.0, 0.0).astype(BF16)
        picked = jnp.dot(picked, feature, preferred_element_type=F32)
        chosen_ref[leaf * K : (leaf + 1) * K, :] = picked.astype(BF16)


def copies_from(value, axis, size):
    copies = jnp.broadcast_to(value[None], (size, *value.shape))
    parts = lax.all_to_all(copies, axis, split_axis=0, concat_axis=0, tiled=True)
    return parts.reshape(size * value.shape[0], *value.shape[1:])


def target_features(me, own, other, notes):
    return pl.pallas_call(
        lookup_kernel,
        out_shape=[jax.ShapeDtypeStruct((LEAF, FEATURES), BF16)] * 5,
        in_specs=[smem()] + [vmem()] * 3,
        out_specs=[vmem()] * 5,
        scratch_shapes=[pltpu.VMEM((2, 1024, 256), BF16)],
        compiler_params=params(),
        name="lookup",
    )(me, own, other, notes)


def source_kernel(*refs):
    half = len(refs) // 2
    for source_ref, out_ref in zip(refs[:half], refs[half:]):
        points = source_ref[...].astype(F32)
        sx, sy = points[0:1], points[1:2]
        size = split3(sx * sx + sy * sy)
        one = jnp.ones_like(sx)
        zero = jnp.zeros_like(sx)
        rows = [-2.0 * sx] * 2 + [-2.0 * sy] * 2 + [one] * 3 + list(size) + [zero] * 6
        out_ref[...] = jnp.concatenate(rows, axis=0).astype(BF16)


def source_features(*blocks):
    width = blocks[0].shape[1]
    return pl.pallas_call(
        source_kernel,
        grid=(1,),
        out_shape=[jax.ShapeDtypeStruct((FEATURES, width), BF16)] * len(blocks),
        in_specs=[pl.BlockSpec((16, width), lambda i: (S // 16, 0))] * len(blocks),
        out_specs=[pl.BlockSpec((FEATURES, width), lambda i: (0, 0))] * len(blocks),
        compiler_params=params(),
        name="source_features",
    )(*blocks)


def sketch_kernel(target_ref, *refs, blocks, begin, finish, chunk):
    features, weights, refs = refs[:blocks], refs[blocks : 2 * blocks], refs[2 * blocks :]
    start_ref, refs = (None, refs) if begin else (refs[0], refs[1:])
    outs, (total_ref, held, feat, sems) = refs[:-4], refs[-4:]
    copies = [
        pltpu.make_async_copy(weight.at[pl.ds(0, S)], held.at[i], sems.at[i])
        for i, weight in enumerate(weights)
    ]
    for copy in copies:
        copy.start()
    for i in range(blocks):
        feat[i] = features[i][...]
    target = target_ref[...]
    width = held.shape[2]
    total_ref[...] = jnp.zeros_like(total_ref) if begin else start_ref[...]
    for i in range(blocks):
        copies[i].wait()
        total = total_ref[...]
        for j in range(width // chunk):
            span = slice(j * chunk, (j + 1) * chunk)
            squared = jnp.dot(target, feat[i, :, span], preferred_element_type=F32)
            panel = jnp.log(squared).astype(BF16)
            total = total + lax.dot_general(
                panel, held[i, :, span], (((1,), (1,)), ((), ())), preferred_element_type=F32
            )
        if i == blocks - 1:
            total = total * (-0.5) if finish else total
            count = total.shape[0] // len(outs)
            for part, out_ref in enumerate(outs):
                out_ref[...] = total[part * count : (part + 1) * count, :].astype(out_ref.dtype)
        else:
            total_ref[...] = total


def sketch_part(target, features, weights, dtypes, start=None, finish=True):
    count, blocks, width = target.shape[0], len(weights), weights[0].shape[1]
    extra = [] if start is None else [start]
    return pl.pallas_call(
        functools.partial(
            sketch_kernel, blocks=blocks, begin=start is None, finish=finish, chunk=256
        ),
        out_shape=[jax.ShapeDtypeStruct((count // len(dtypes), S), dtype) for dtype in dtypes],
        in_specs=[vmem()] * (1 + blocks)
        + [pl.BlockSpec(memory_space=pl.ANY)] * blocks
        + [vmem()] * len(extra),
        out_specs=[vmem()] * len(dtypes),
        scratch_shapes=[
            pltpu.VMEM((count, S), F32),
            pltpu.VMEM((blocks, S, width), BF16),
            pltpu.VMEM((blocks, FEATURES, width), BF16),
            pltpu.SemaphoreType.DMA((blocks,)),
        ],
        compiler_params=params(),
        name="sketch",
    )(target, *features, *weights, *extra)


def swap_cores(value):
    return lax.ppermute(value, "k", [(0, 1), (1, 0)])


def along_z(step, forward):
    pairs = []
    for sz in range(NZ):
        for sk in range(NK):
            other = (sz + (step if sz % 2 else -step)) % NZ
            pair = (sz * NK + sk, other * NK + sk)
            pairs.append(pair if forward else pair[::-1])
    return pairs


def take_rows(pivot_ref, source_ref, out_ref):
    def body(step, carry):
        for i in range(8):
            spot = step * 8 + i
            out_ref[pl.ds(spot, 1), :] = source_ref[pl.ds(pivot_ref[spot], 1), :]
        return carry

    lax.fori_loop(0, K // 8, body, 0)


def choose_kernel(pivot_ref, own_ref, other_ref, chosen_ref, both):
    both[0:K, :] = own_ref[...]
    both[K:, :] = other_ref[...]
    take_rows(pivot_ref, both, chosen_ref)


def choose(pivots, own, other):
    return pl.pallas_call(
        choose_kernel,
        out_shape=jax.ShapeDtypeStruct((K, S), F32),
        in_specs=[smem(), vmem(), vmem()],
        out_specs=vmem(),
        scratch_shapes=[pltpu.VMEM((2 * K, S), F32)],
        compiler_params=params(),
        name="choose",
    )(pivots, own, other)


def eliminate(matrix, i):
    lane = lax.broadcasted_iota(jnp.int32, (1, K), 1)
    line = lax.broadcasted_iota(jnp.int32, (K, K), 0)
    columns = [jnp.broadcast_to(matrix[:, i + t : i + t + 1], (K, K)) for t in range(PIVOT)]
    (p, q), (r, s) = [[column[i + t : i + t + 1, :] for column in columns] for t in range(PIVOT)]
    rows = [
        matrix[i + t : i + t + 1, :] - jnp.where(lane == i + t, 1.0, 0.0) for t in range(PIVOT)
    ]
    scale = 1.0 / (p * s - q * r)
    rows = [(s * rows[0] - q * rows[1]) * scale, (p * rows[1] - r * rows[0]) * scale]
    for t, row in enumerate(rows):
        matrix = matrix - (columns[t] - jnp.where(line == i + t, 1.0, 0.0)) * row
    return matrix


def dot_rows(left, right):
    return lax.dot_general(
        left,
        right,
        (((1,), (1,)), ((), ())),
        precision=lax.Precision.HIGHEST,
        preferred_element_type=F32,
    )


def tree_kernel(
    pivot_ref, spot_ref, c0_ref, c1_ref, c2_ref, o2_ref,
    inverse_ref, one_ref, two_ref, three_ref, root_ref,
    both, c3_ref, work,
):
    both[0:K, :] = c2_ref[...]
    both[K:, :] = o2_ref[...]
    take_rows(pivot_ref, both, c3_ref)
    root_ref[...] = c3_ref[pl.ds(pl.multiple_of(spot_ref[2], 16), 16), :]
    lane = lax.broadcasted_iota(jnp.int32, (K, K), 1)
    line = lax.broadcasted_iota(jnp.int32, (K, K), 0)
    eye = lane == line
    chosen = (c0_ref, c1_ref, c2_ref, c3_ref)
    scales = []
    for level, ref in enumerate(chosen):
        rows = ref[...]
        gram = dot_rows(rows, rows)
        trace = jnp.sum(jnp.where(eye, gram, 0.0), axis=1, keepdims=True)
        trace = jnp.sum(trace, axis=0, keepdims=True)
        scale = 1.0 / (trace / K + 1e-06)
        scales.append(scale)
        work[level] = gram * scale + jnp.where(eye, RIDGE, 0.0)

    def block(step, carry):
        values = [work[level] for level in range(4)]
        for i in range(0, BLOCK, PIVOT):
            values = [eliminate(value, i) for value in values]
        for level in range(4):
            turned = pltpu.roll(values[level], K - BLOCK, 1)
            work[level, 0 : K - BLOCK, :] = turned[BLOCK:, :]
            work[level, K - BLOCK : K, :] = turned[:BLOCK, :]
        return carry

    lax.fori_loop(0, K // BLOCK, block, 0)
    shares = (
        None,
        c0_ref[...],
        c1_ref[pl.ds(pl.multiple_of(spot_ref[0], 64), 64), :],
        c2_ref[pl.ds(pl.multiple_of(spot_ref[1], 32), 32), :],
    )
    outs = (inverse_ref, one_ref, two_ref, three_ref)
    for level in range(4):
        inverse = (jnp.where(eye, 2.0, 0.0) - work[level]) * scales[level]
        if level > 0:
            right = dot_rows(shares[level], chosen[level][...])
            inverse = jnp.dot(
                right, inverse, precision=lax.Precision.HIGHEST, preferred_element_type=F32
            )
        outs[level][...] = inverse


def leaf_kernel(own_ref, a_ref, b_ref, c_ref, c0_ref, inverse_ref, out_ref):
    others = a_ref[...].astype(F32) + b_ref[...].astype(F32) + c_ref[...].astype(F32)
    right = dot_rows(own_ref[...] + others, c0_ref[...])
    out_ref[...] = jnp.dot(
        right, inverse_ref[...], precision=lax.Precision.HIGHEST, preferred_element_type=F32
    )


def body(targets, sources, omega, tree_order, leaf_pivots, pivots_one, pivots_two, pivots_three):
    y, x, z, k = (lax.axis_index(axis) for axis in ALL_AXES)
    leaf = ((y * NX + x) * NZ + z) * NK + k
    bits = (k, z & 1, (z >> 1) & 1)
    tables = (pivots_one, pivots_two, pivots_three)
    pivots = [
        lax.dynamic_index_in_dim(table, leaf >> level + 1, 0, keepdims=False)
        ^ (bits[level] * K).astype(jnp.int32)
        for level, table in enumerate(tables)
    ]

    spots = jnp.stack([k * 64, ((z & 1) * 2 + k) * 32, ((z & 3) * 2 + k) * 16]).astype(jnp.int32)
    ahead = jnp.where(z & 1, 1, -1)
    me = jnp.stack([k] + [(z + d * ahead) & 7 for d in range(4)]).astype(jnp.int32)

    lines = targets.reshape(2, 4, 128).transpose(1, 0, 2).reshape(8, 128)
    notes = [tree_order.reshape(4, 128).astype(F32), leaf_pivots.astype(F32), jnp.zeros((3, 128))]
    plane = copies_from(jnp.concatenate([lines, *notes], axis=0), "z", NZ)
    pad = jnp.zeros((14, sources.shape[1]), BF16)
    block = jnp.concatenate([omega, sources, pad], axis=0)
    plane, block, pivots, spots, me = lax.optimization_barrier((plane, block, pivots, spots, me))
    far = lax.ppermute(block, "z", [(s, s ^ 1) for s in range(NZ)])
    weights = [block, swap_cores(block)]
    features = source_features(*weights)
    plane = plane.reshape(NZ, 16, 128)
    table = copies_from(plane[:, :8].reshape(NZ * 8, 128), ("y", "x"), NY * NX)
    *leaves, chosen = target_features(me, table, swap_cores(table), plane[:, 8:])
    far, leaves, chosen = lax.optimization_barrier((far, leaves, chosen))
    far = [far, swap_cores(far)]

    def give(part, d):
        return lax.ppermute(part, ZK, along_z(d, True))

    (near,) = sketch_part(chosen, features, weights, [F32], finish=False)
    far_features = source_features(*far)
    c0, *parts = sketch_part(
        chosen, far_features, far, [F32] + [BF16] * 3, start=near
    )
    parts = [give(parts[d - 1], d) for d in (3, 2, 1)]
    weights, features = weights + far, features + far_features
    (third,) = sketch_part(leaves[3], features, weights, [BF16])
    third, parts = lax.optimization_barrier((third, parts))
    third = give(third, 3)
    c0 = c0 + (parts[0].astype(F32) + parts[1].astype(F32) + parts[2].astype(F32))
    c1 = choose(pivots[0], c0, swap_cores(c0))
    c1, leaf = lax.optimization_barrier((c1, leaves[2]))
    other1 = lax.ppermute(c1, "z", [(s, s ^ 1) for s in range(NZ)])
    (second,) = sketch_part(leaf, features, weights, [BF16])
    second, other1 = lax.optimization_barrier((second, other1))
    second = give(second, 2)
    c2 = choose(pivots[1], c1, other1)
    c2, third, leaf = lax.optimization_barrier((c2, third, leaves[1]))
    other2 = lax.ppermute(c2, "z", [(s, s ^ 2) for s in range(NZ)])
    (first,) = sketch_part(leaf, features, weights, [BF16])
    first, leaf = lax.optimization_barrier((first, leaves[0]))
    first = give(first, 1)
    (own,) = sketch_part(leaf, features, weights, [F32])
    own, second, other2 = lax.optimization_barrier((own, second, other2))
    inverse, one_out, two_out, three_out, root = pl.pallas_call(
        tree_kernel,
        out_shape=[
            jax.ShapeDtypeStruct((K, K), F32),
            jax.ShapeDtypeStruct((K, K), F32),
            jax.ShapeDtypeStruct((K // 2, K), F32),
            jax.ShapeDtypeStruct((K // 4, K), F32),
            jax.ShapeDtypeStruct((K // 8, S), F32),
        ],
        in_specs=[smem()] * 2 + [vmem()] * 4,
        out_specs=[vmem()] * 5,
        scratch_shapes=[
            pltpu.VMEM((2 * K, S), F32),
            pltpu.VMEM((K, S), F32),
            pltpu.VMEM((4, K, K), F32),
        ],
        compiler_params=params(),
        name="tree",
    )(pivots[2], spots, c0, c1, c2, other2)
    leaf_out = pl.pallas_call(
        leaf_kernel,
        out_shape=jax.ShapeDtypeStruct((LEAF, K), F32),
        in_specs=[vmem()] * 6,
        out_specs=vmem(),
        compiler_params=params(),
        name="leaf_interp",
    )(own, third, second, first, c0, inverse)
    return leaf_out, one_out, two_out, three_out, root


def solution(mesh):
    finer = Mesh(mesh.devices.reshape(NY, NX, NZ, NK), ALL_AXES)
    col = ("z", "k")
    placed = (
        P(None, ALL_AXES),
        P(None, col),
        P(None, col),
        P(ALL_AXES),
        P(ALL_AXES, None),
        P(),
        P(),
        P(),
    )
    return jax.shard_map(
        body,
        mesh=finer,
        in_specs=placed,
        out_specs=(P(ALL_AXES, None),) * 5,
        check_vma=False,
    )
```

```python
import functools

import jax
import jax.numpy as jnp
from jax import lax
from jax.experimental import pallas as pl
from jax.experimental.pallas import tpu as pltpu
from jax.sharding import Mesh
from jax.sharding import PartitionSpec as P

LEAF = 512
S = 256
K = 128
FEATURES = 16
BLOCK = 32
RIDGE = 0.1
DELTA_SQUARED = 0.0001
ALL_AXES = ("y", "x", "z", "k")
ZK = ("z", "k")
NY, NX, NZ, NK = 4, 4, 8, 2
F32 = jnp.float32
BF16 = jnp.bfloat16
VMEM_LIMIT = 40 << 20


def params():
    return pltpu.CompilerParams(vmem_limit_bytes=VMEM_LIMIT)


def smem():
    return pl.BlockSpec(memory_space=pltpu.SMEM)


def vmem():
    return pl.BlockSpec(memory_space=pltpu.VMEM)


def split3(value):
    high = value.astype(BF16).astype(F32)
    rest = value - high
    middle = rest.astype(BF16).astype(F32)
    low = (rest - middle).astype(BF16).astype(F32)
    return high, middle, low


def lookup_kernel(me_ref, own_ref, other_ref, note_ref, *refs):
    outs, chosen_ref, turned = refs[:4], refs[4], refs[5]
    for side, table_ref in enumerate((own_ref, other_ref)):
        for coord in range(2):
            values = jnp.transpose(table_ref[pl.ds(coord, LEAF, stride=2), :])
            for half, part in enumerate(split3(values)[:2]):
                row = (2 * half + coord) * 128
                turned[row : row + 128, side * LEAF : (side + 1) * LEAF] = part.astype(BF16)
    core = me_ref[0]
    line = lax.broadcasted_iota(jnp.int32, (1024, LEAF), 0)
    place = lax.broadcasted_iota(jnp.int32, (128, LEAF), 0)
    spot = lax.broadcasted_iota(jnp.int32, (LEAF, K), 0)
    one = jnp.ones((3, LEAF), F32)
    zero = jnp.zeros((6, LEAF), F32)
    for leaf, out_ref in enumerate(outs):
        note = note_ref[me_ref[1 + leaf]].astype(jnp.int32)
        index = jnp.concatenate([note[i : i + 1, :] for i in range(4)], axis=1)
        row = (((index >> 9) & 1) ^ core) * LEAF + (index >> 10) * 4 + ((index >> 7) & 3)
        hot = jnp.where(line == row, 1.0, 0.0).astype(BF16)
        rows = jnp.dot(turned[...], hot, preferred_element_type=F32)
        rows = rows[:256] + rows[256:]
        mask = place == (index & 127)
        tx = jnp.sum(jnp.where(mask, rows[:128], 0.0), axis=0, keepdims=True)
        ty = jnp.sum(jnp.where(mask, rows[128:], 0.0), axis=0, keepdims=True)
        parts = list(split3(tx)[:2]) + list(split3(ty)[:2])
        parts += list(split3(tx * tx + (ty * ty + DELTA_SQUARED)))
        feature = jnp.concatenate(parts + [one, zero], axis=0)
        out_ref[...] = jnp.transpose(feature).astype(BF16)
        picked = jnp.where(spot == note[4:5, :], 1.0, 0.0).astype(BF16)
        picked = jnp.dot(feature.astype(BF16), picked, preferred_element_type=F32)
        chosen_ref[leaf * K : (leaf + 1) * K, :] = jnp.transpose(picked).astype(BF16)


def pack_kernel(target_ref, order_ref, pivot_ref, out_ref):
    rows = [
        target_ref[coord : coord + 1, i * 128 : (i + 1) * 128] for i in range(4) for coord in range(2)
    ]
    order = order_ref[...].astype(F32)
    rows += [order[:, i * 128 : (i + 1) * 128] for i in range(4)]
    rows += [pivot_ref[...].astype(F32), jnp.zeros((3, 128), F32)]
    rows = jnp.concatenate(rows, axis=0)
    for i in range(out_ref.shape[0]):
        out_ref[i] = rows


def copies_from(value, axis, size):
    copies = jnp.broadcast_to(value[None], (size, *value.shape))
    parts = lax.all_to_all(copies, axis, split_axis=0, concat_axis=0, tiled=True)
    return parts.reshape(size * value.shape[0], *value.shape[1:])


def target_features(me, own, other, notes):
    return pl.pallas_call(
        lookup_kernel,
        out_shape=[jax.ShapeDtypeStruct((LEAF, FEATURES), BF16)] * 5,
        in_specs=[smem()] + [vmem()] * 3,
        out_specs=[vmem()] * 5,
        scratch_shapes=[pltpu.VMEM((512, 1024), BF16)],
        compiler_params=params(),
        name="lookup",
    )(me, own, other, notes)


def source_kernel(*refs):
    half = len(refs) // 2
    for source_ref, out_ref in zip(refs[:half], refs[half:]):
        points = source_ref[...].astype(F32)
        sx, sy = points[0:1], points[1:2]
        size = split3(sx * sx + sy * sy)
        one = jnp.ones_like(sx)
        zero = jnp.zeros_like(sx)
        rows = [-2.0 * sx] * 2 + [-2.0 * sy] * 2 + [one] * 3 + list(size) + [zero] * 6
        out_ref[...] = jnp.concatenate(rows, axis=0).astype(BF16)


def source_features(*blocks):
    width = blocks[0].shape[1]
    return pl.pallas_call(
        source_kernel,
        grid=(1,),
        out_shape=[jax.ShapeDtypeStruct((FEATURES, width), BF16)] * len(blocks),
        in_specs=[pl.BlockSpec((16, width), lambda i: (S // 16, 0))] * len(blocks),
        out_specs=[pl.BlockSpec((FEATURES, width), lambda i: (0, 0))] * len(blocks),
        compiler_params=params(),
        name="source_features",
    )(*blocks)


def sketch_kernel(target_ref, *refs, blocks, begin, finish, chunk):
    features, weights, refs = refs[:blocks], refs[blocks : 2 * blocks], refs[2 * blocks :]
    start_ref, refs = (None, refs) if begin else (refs[0], refs[1:])
    outs, (total_ref, held, feat, sems) = refs[:-4], refs[-4:]
    copies = [
        pltpu.make_async_copy(weight.at[pl.ds(0, S)], held.at[i], sems.at[i])
        for i, weight in enumerate(weights)
    ]
    for copy in copies:
        copy.start()
    for i in range(blocks):
        feat[i] = features[i][...]
    target = target_ref[...]
    width = held.shape[2]
    total_ref[...] = jnp.zeros_like(total_ref) if begin else start_ref[...]
    for i in range(blocks):
        copies[i].wait()
        total = total_ref[...]
        for j in range(width // chunk):
            span = slice(j * chunk, (j + 1) * chunk)
            squared = jnp.dot(target, feat[i, :, span], preferred_element_type=F32)
            panel = jnp.log(squared).astype(BF16)
            total = total + lax.dot_general(
                panel, held[i, :, span], (((1,), (1,)), ((), ())), preferred_element_type=F32
            )
        if i == blocks - 1:
            total = total * (-0.5) if finish else total
            count = total.shape[0] // len(outs)
            for part, out_ref in enumerate(outs):
                out_ref[...] = total[part * count : (part + 1) * count, :].astype(out_ref.dtype)
        else:
            total_ref[...] = total


def sketch_part(target, features, weights, dtypes, start=None, finish=True):
    count, blocks, width = target.shape[0], len(weights), weights[0].shape[1]
    extra = [] if start is None else [start]
    return pl.pallas_call(
        functools.partial(
            sketch_kernel, blocks=blocks, begin=start is None, finish=finish, chunk=256
        ),
        out_shape=[jax.ShapeDtypeStruct((count // len(dtypes), S), dtype) for dtype in dtypes],
        in_specs=[vmem()] * (1 + blocks)
        + [pl.BlockSpec(memory_space=pl.ANY)] * blocks
        + [vmem()] * len(extra),
        out_specs=[vmem()] * len(dtypes),
        scratch_shapes=[
            pltpu.VMEM((count, S), F32),
            pltpu.VMEM((blocks, S, width), BF16),
            pltpu.VMEM((blocks, FEATURES, width), BF16),
            pltpu.SemaphoreType.DMA((blocks,)),
        ],
        compiler_params=params(),
        name="sketch",
    )(target, *features, *weights, *extra)


def swap_cores(value):
    return lax.ppermute(value, "k", [(0, 1), (1, 0)])


def along_z(step, forward):
    pairs = []
    for sz in range(NZ):
        for sk in range(NK):
            other = (sz + (step if sz % 2 else -step)) % NZ
            pair = (sz * NK + sk, other * NK + sk)
            pairs.append(pair if forward else pair[::-1])
    return pairs


def take_rows(pivot_ref, source_ref, out_ref):
    def body(step, carry):
        for i in range(8):
            spot = step * 8 + i
            out_ref[pl.ds(spot, 1), :] = source_ref[pl.ds(pivot_ref[spot], 1), :]
        return carry

    lax.fori_loop(0, K // 8, body, 0)


def choose_kernel(pivot_ref, own_ref, other_ref, chosen_ref, both):
    both[0:K, :] = own_ref[...]
    both[K:, :] = other_ref[...]
    take_rows(pivot_ref, both, chosen_ref)


def choose(pivots, own, other):
    return pl.pallas_call(
        choose_kernel,
        out_shape=jax.ShapeDtypeStruct((K, S), F32),
        in_specs=[smem(), vmem(), vmem()],
        out_specs=vmem(),
        scratch_shapes=[pltpu.VMEM((2 * K, S), F32)],
        compiler_params=params(),
        name="choose",
    )(pivots, own, other)


def eliminate(panel, i):
    lane = lax.broadcasted_iota(jnp.int32, (1, K), 1)
    line = lax.broadcasted_iota(jnp.int32, (BLOCK, K), 0)
    columns = [jnp.broadcast_to(panel[:, i + t : i + t + 1], (BLOCK, K)) for t in range(2)]
    (p, q), (r, s) = [[column[i + t : i + t + 1, :] for column in columns] for t in range(2)]
    rows = [panel[i + t : i + t + 1, :] - jnp.where(lane == i + t, 1.0, 0.0) for t in range(2)]
    scale = 1.0 / (p * s - q * r)
    rows = [(s * rows[0] - q * rows[1]) * scale, (p * rows[1] - r * rows[0]) * scale]
    for t, row in enumerate(rows):
        panel = panel - (columns[t] - jnp.where(line == i + t, 1.0, 0.0)) * row
    return panel


def invert(work):
    count = work.shape[0]
    line = lax.broadcasted_iota(jnp.int32, (BLOCK, K), 0)
    lane = lax.broadcasted_iota(jnp.int32, (BLOCK, K), 1)
    eye = jnp.where(line == lane, 1.0, 0.0)

    def block(step, carry):
        panels = [work[m, 0:BLOCK, :] for m in range(count)]
        before = [panel - eye for panel in panels]
        for i in range(0, BLOCK, 2):
            panels = [eliminate(panel, i) for panel in panels]
        for m in range(count):
            left, right = split3(before[m]), split3(panels[m] - eye)
            pairs = [(0, 0), (0, 1), (1, 0), (1, 1), (0, 2), (2, 0)]
            left = jnp.concatenate([left[i] for i, _ in pairs], axis=0).astype(BF16)
            right = jnp.concatenate([right[j] for _, j in pairs], axis=0).astype(BF16)
            update = lax.dot_general(
                left, right, (((0,), (0,)), ((), ())), preferred_element_type=F32
            )
            turned = pltpu.roll(work[m] - update, K - BLOCK, 1)
            work[m, 0 : K - BLOCK, :] = turned[BLOCK:, :]
            work[m, K - BLOCK : K, :] = turned[:BLOCK, :]
        return carry

    lax.fori_loop(0, K // BLOCK, block, 0)


def dot_rows(left, right):
    return lax.dot_general(
        left,
        right,
        (((1,), (1,)), ((), ())),
        precision=lax.Precision.HIGHEST,
        preferred_element_type=F32,
    )


def tree_kernel(
    pivot_ref, spot_ref, c0_ref, c1_ref, c2_ref, o2_ref,
    inverse_ref, one_ref, two_ref, three_ref, root_ref,
    both, c3_ref, work,
):
    both[0:K, :] = c2_ref[...]
    both[K:, :] = o2_ref[...]
    take_rows(pivot_ref, both, c3_ref)
    root_ref[...] = c3_ref[pl.ds(pl.multiple_of(spot_ref[2], 16), 16), :]
    lane = lax.broadcasted_iota(jnp.int32, (K, K), 1)
    line = lax.broadcasted_iota(jnp.int32, (K, K), 0)
    eye = lane == line
    chosen = (c0_ref, c1_ref, c2_ref, c3_ref)
    scales = []
    for level, ref in enumerate(chosen):
        rows = ref[...]
        gram = dot_rows(rows, rows)
        trace = jnp.sum(jnp.where(eye, gram, 0.0), axis=1, keepdims=True)
        trace = jnp.sum(trace, axis=0, keepdims=True)
        scale = 1.0 / (trace / K + 1e-06)
        scales.append(scale)
        work[level] = gram * scale + jnp.where(eye, RIDGE, 0.0)

    invert(work)
    shares = (
        None,
        c0_ref[...],
        c1_ref[pl.ds(pl.multiple_of(spot_ref[0], 64), 64), :],
        c2_ref[pl.ds(pl.multiple_of(spot_ref[1], 32), 32), :],
    )
    outs = (inverse_ref, one_ref, two_ref, three_ref)
    for level in range(4):
        inverse = (jnp.where(eye, 2.0, 0.0) - work[level]) * scales[level]
        if level > 0:
            right = dot_rows(shares[level], chosen[level][...])
            inverse = jnp.dot(
                right, inverse, precision=lax.Precision.HIGHEST, preferred_element_type=F32
            )
        outs[level][...] = inverse


def leaf_kernel(own_ref, a_ref, b_ref, c_ref, c0_ref, inverse_ref, out_ref):
    others = a_ref[...].astype(F32) + b_ref[...].astype(F32) + c_ref[...].astype(F32)
    right = dot_rows(own_ref[...] + others, c0_ref[...])
    out_ref[...] = jnp.dot(
        right, inverse_ref[...], precision=lax.Precision.HIGHEST, preferred_element_type=F32
    )


def body(targets, sources, omega, tree_order, leaf_pivots, pivots_one, pivots_two, pivots_three):
    y, x, z, k = (lax.axis_index(axis) for axis in ALL_AXES)
    leaf = ((y * NX + x) * NZ + z) * NK + k
    bits = (k, z & 1, (z >> 1) & 1)
    tables = (pivots_one, pivots_two, pivots_three)
    pivots = [
        lax.dynamic_index_in_dim(table, leaf >> level + 1, 0, keepdims=False)
        ^ (bits[level] * K).astype(jnp.int32)
        for level, table in enumerate(tables)
    ]

    spots = jnp.stack([k * 64, ((z & 1) * 2 + k) * 32, ((z & 3) * 2 + k) * 16]).astype(jnp.int32)
    ahead = jnp.where(z & 1, 1, -1)
    me = jnp.stack([k] + [(z + d * ahead) & 7 for d in range(4)]).astype(jnp.int32)

    plane = pl.pallas_call(
        pack_kernel,
        out_shape=jax.ShapeDtypeStruct((NZ, 16, 128), F32),
        in_specs=[vmem()] * 3,
        out_specs=vmem(),
        compiler_params=params(),
        name="pack",
    )(targets, tree_order.reshape(1, LEAF), leaf_pivots)
    plane = lax.all_to_all(plane, "z", split_axis=0, concat_axis=0, tiled=True)
    pad = jnp.zeros((14, sources.shape[1]), BF16)
    block = jnp.concatenate([omega, sources, pad], axis=0)
    plane, block, pivots, spots, me = lax.optimization_barrier((plane, block, pivots, spots, me))
    far = lax.ppermute(block, "z", [(s, s ^ 1) for s in range(NZ)])
    weights = [block, swap_cores(block)]
    features = source_features(*weights)
    table = copies_from(plane[:, :8].reshape(NZ * 8, 128), ("y", "x"), NY * NX)
    *leaves, chosen = target_features(me, table, swap_cores(table), plane[:, 8:])
    far, leaves, chosen = lax.optimization_barrier((far, leaves, chosen))
    far = [far, swap_cores(far)]

    def give(part, d):
        return lax.ppermute(part, ZK, along_z(d, True))

    (near,) = sketch_part(chosen, features, weights, [F32], finish=False)
    far_features = source_features(*far)
    c0, *parts = sketch_part(
        chosen, far_features, far, [F32] + [BF16] * 3, start=near
    )
    parts = [give(parts[d - 1], d) for d in (3, 2, 1)]
    weights, features = weights + far, features + far_features
    (third,) = sketch_part(leaves[3], features, weights, [BF16])
    third, parts = lax.optimization_barrier((third, parts))
    third = give(third, 3)
    c0 = c0 + (parts[0].astype(F32) + parts[1].astype(F32) + parts[2].astype(F32))
    c1 = choose(pivots[0], c0, swap_cores(c0))
    c1, leaf = lax.optimization_barrier((c1, leaves[2]))
    other1 = lax.ppermute(c1, "z", [(s, s ^ 1) for s in range(NZ)])
    (second,) = sketch_part(leaf, features, weights, [BF16])
    second, other1 = lax.optimization_barrier((second, other1))
    second = give(second, 2)
    c2 = choose(pivots[1], c1, other1)
    c2, third, leaf = lax.optimization_barrier((c2, third, leaves[1]))
    other2 = lax.ppermute(c2, "z", [(s, s ^ 2) for s in range(NZ)])
    (first,) = sketch_part(leaf, features, weights, [BF16])
    first, leaf = lax.optimization_barrier((first, leaves[0]))
    first = give(first, 1)
    (own,) = sketch_part(leaf, features, weights, [F32])
    own, second, other2 = lax.optimization_barrier((own, second, other2))
    inverse, one_out, two_out, three_out, root = pl.pallas_call(
        tree_kernel,
        out_shape=[
            jax.ShapeDtypeStruct((K, K), F32),
            jax.ShapeDtypeStruct((K, K), F32),
            jax.ShapeDtypeStruct((K // 2, K), F32),
            jax.ShapeDtypeStruct((K // 4, K), F32),
            jax.ShapeDtypeStruct((K // 8, S), F32),
        ],
        in_specs=[smem()] * 2 + [vmem()] * 4,
        out_specs=[vmem()] * 5,
        scratch_shapes=[
            pltpu.VMEM((2 * K, S), F32),
            pltpu.VMEM((K, S), F32),
            pltpu.VMEM((4, K, K), F32),
        ],
        compiler_params=params(),
        name="tree",
    )(pivots[2], spots, c0, c1, c2, other2)
    leaf_out = pl.pallas_call(
        leaf_kernel,
        out_shape=jax.ShapeDtypeStruct((LEAF, K), F32),
        in_specs=[vmem()] * 6,
        out_specs=vmem(),
        compiler_params=params(),
        name="leaf_interp",
    )(own, third, second, first, c0, inverse)
    return leaf_out, one_out, two_out, three_out, root


def solution(mesh):
    finer = Mesh(mesh.devices.reshape(NY, NX, NZ, NK), ALL_AXES)
    col = ("z", "k")
    placed = (
        P(None, ALL_AXES),
        P(None, col),
        P(None, col),
        P(ALL_AXES),
        P(ALL_AXES, None),
        P(),
        P(),
        P(),
    )
    return jax.shard_map(
        body,
        mesh=finer,
        in_specs=placed,
        out_specs=(P(ALL_AXES, None),) * 5,
        check_vma=False,
    )
```

```python
import functools

import jax
import jax.numpy as jnp
from jax import lax
from jax.experimental import pallas as pl
from jax.experimental.pallas import tpu as pltpu
from jax.sharding import Mesh
from jax.sharding import PartitionSpec as P

LEAF = 512
S = 256
K = 128
FEATURES = 16
BLOCK = 32
RIDGE = 0.1
DELTA_SQUARED = 0.0001
ALL_AXES = ("y", "x", "z", "k")
ZK = ("z", "k")
NY, NX, NZ, NK = 4, 4, 8, 2
F32 = jnp.float32
BF16 = jnp.bfloat16
VMEM_LIMIT = 40 << 20


def params():
    return pltpu.CompilerParams(vmem_limit_bytes=VMEM_LIMIT)


def smem():
    return pl.BlockSpec(memory_space=pltpu.SMEM)


def vmem():
    return pl.BlockSpec(memory_space=pltpu.VMEM)


def split3(value):
    high = value.astype(BF16).astype(F32)
    rest = value - high
    middle = rest.astype(BF16).astype(F32)
    low = (rest - middle).astype(BF16).astype(F32)
    return high, middle, low


def lookup_kernel(me_ref, own_ref, other_ref, note_ref, *refs):
    outs, chosen_ref, turned = refs[:4], refs[4], refs[5]
    for side, table_ref in enumerate((own_ref, other_ref)):
        for coord in range(2):
            values = jnp.transpose(table_ref[pl.ds(coord, LEAF, stride=2), :])
            for half, part in enumerate(split3(values)[:2]):
                row = (2 * half + coord) * 128
                turned[row : row + 128, side * LEAF : (side + 1) * LEAF] = part.astype(BF16)
    core = me_ref[0]
    line = lax.broadcasted_iota(jnp.int32, (1024, LEAF), 0)
    place = lax.broadcasted_iota(jnp.int32, (128, LEAF), 0)
    spot = lax.broadcasted_iota(jnp.int32, (LEAF, K), 0)
    one = jnp.ones((3, LEAF), F32)
    zero = jnp.zeros((6, LEAF), F32)
    for leaf, out_ref in enumerate(outs):
        note = note_ref[me_ref[1 + leaf]].astype(jnp.int32)
        index = jnp.concatenate([note[i : i + 1, :] for i in range(4)], axis=1)
        row = (((index >> 9) & 1) ^ core) * LEAF + (index >> 10) * 4 + ((index >> 7) & 3)
        hot = jnp.where(line == row, 1.0, 0.0).astype(BF16)
        rows = jnp.dot(turned[...], hot, preferred_element_type=F32)
        rows = rows[:256] + rows[256:]
        mask = place == (index & 127)
        tx = jnp.sum(jnp.where(mask, rows[:128], 0.0), axis=0, keepdims=True)
        ty = jnp.sum(jnp.where(mask, rows[128:], 0.0), axis=0, keepdims=True)
        parts = list(split3(tx)[:2]) + list(split3(ty)[:2])
        parts += list(split3(tx * tx + (ty * ty + DELTA_SQUARED)))
        feature = jnp.concatenate(parts + [one, zero], axis=0)
        out_ref[...] = jnp.transpose(feature).astype(BF16)
        picked = jnp.where(spot == note[4:5, :], 1.0, 0.0).astype(BF16)
        picked = jnp.dot(feature.astype(BF16), picked, preferred_element_type=F32)
        chosen_ref[leaf * K : (leaf + 1) * K, :] = jnp.transpose(picked).astype(BF16)


def pack_kernel(target_hbm, order_hbm, pivot_hbm, out_ref, target_ref, order_ref, pivot_ref, sems):
    pairs = ((target_hbm, target_ref), (order_hbm, order_ref), (pivot_hbm, pivot_ref))
    copies = [
        pltpu.make_async_copy(source, held, sems.at[i]) for i, (source, held) in enumerate(pairs)
    ]
    for copy in copies:
        copy.start()
    for copy in copies:
        copy.wait()
    rows = [
        target_ref[coord : coord + 1, i * 128 : (i + 1) * 128] for i in range(4) for coord in range(2)
    ]
    order = order_ref[...].astype(F32)
    rows += [order[:, i * 128 : (i + 1) * 128] for i in range(4)]
    rows += [pivot_ref[...].astype(F32), jnp.zeros((3, 128), F32)]
    rows = jnp.concatenate(rows, axis=0)
    for i in range(out_ref.shape[0]):
        out_ref[i] = rows


def copies_from(value, axis, size):
    copies = jnp.broadcast_to(value[None], (size, *value.shape))
    parts = lax.all_to_all(copies, axis, split_axis=0, concat_axis=0, tiled=True)
    return parts.reshape(size * value.shape[0], *value.shape[1:])


def target_features(me, own, other, notes):
    return pl.pallas_call(
        lookup_kernel,
        out_shape=[jax.ShapeDtypeStruct((LEAF, FEATURES), BF16)] * 5,
        in_specs=[smem()] + [vmem()] * 3,
        out_specs=[vmem()] * 5,
        scratch_shapes=[pltpu.VMEM((512, 1024), BF16)],
        compiler_params=params(),
        name="lookup",
    )(me, own, other, notes)


def source_kernel(*refs):
    half = len(refs) // 2
    for source_ref, out_ref in zip(refs[:half], refs[half:]):
        points = source_ref[...].astype(F32)
        sx, sy = points[0:1], points[1:2]
        size = split3(sx * sx + sy * sy)
        one = jnp.ones_like(sx)
        zero = jnp.zeros_like(sx)
        rows = [-2.0 * sx] * 2 + [-2.0 * sy] * 2 + [one] * 3 + list(size) + [zero] * 6
        out_ref[...] = jnp.concatenate(rows, axis=0).astype(BF16)


def source_features(*blocks):
    width = blocks[0].shape[1]
    return pl.pallas_call(
        source_kernel,
        grid=(1,),
        out_shape=[jax.ShapeDtypeStruct((FEATURES, width), BF16)] * len(blocks),
        in_specs=[pl.BlockSpec((16, width), lambda i: (S // 16, 0))] * len(blocks),
        out_specs=[pl.BlockSpec((FEATURES, width), lambda i: (0, 0))] * len(blocks),
        compiler_params=params(),
        name="source_features",
    )(*blocks)


def sketch_kernel(target_ref, *refs, blocks, begin, finish, chunk):
    features, weights, refs = refs[:blocks], refs[blocks : 2 * blocks], refs[2 * blocks :]
    start_ref, refs = (None, refs) if begin else (refs[0], refs[1:])
    outs, total_ref = refs[:-1], refs[-1]
    target = target_ref[...]
    width = features[0].shape[1]
    total_ref[...] = jnp.zeros_like(total_ref) if begin else start_ref[...]
    for i in range(blocks):
        total = total_ref[...]
        for j in range(width // chunk):
            span = slice(j * chunk, (j + 1) * chunk)
            squared = jnp.dot(target, features[i][:, span], preferred_element_type=F32)
            panel = jnp.log(squared).astype(BF16)
            total = total + lax.dot_general(
                panel,
                weights[i][0:S, span],
                (((1,), (1,)), ((), ())),
                preferred_element_type=F32,
            )
        if i == blocks - 1:
            total = total * (-0.5) if finish else total
            count = total.shape[0] // len(outs)
            for part, out_ref in enumerate(outs):
                out_ref[...] = total[part * count : (part + 1) * count, :].astype(out_ref.dtype)
        else:
            total_ref[...] = total


def sketch_part(target, features, weights, dtypes, start=None, finish=True):
    count, blocks = target.shape[0], len(weights)
    extra = [] if start is None else [start]
    return pl.pallas_call(
        functools.partial(
            sketch_kernel, blocks=blocks, begin=start is None, finish=finish, chunk=256
        ),
        out_shape=[jax.ShapeDtypeStruct((count // len(dtypes), S), dtype) for dtype in dtypes],
        in_specs=[vmem()] * (1 + 2 * blocks + len(extra)),
        out_specs=[vmem()] * len(dtypes),
        scratch_shapes=[pltpu.VMEM((count, S), F32)],
        compiler_params=params(),
        name="sketch",
    )(target, *features, *weights, *extra)


def swap_cores(value):
    return lax.ppermute(value, "k", [(0, 1), (1, 0)])


def along_z(step, forward):
    pairs = []
    for sz in range(NZ):
        for sk in range(NK):
            other = (sz + (step if sz % 2 else -step)) % NZ
            pair = (sz * NK + sk, other * NK + sk)
            pairs.append(pair if forward else pair[::-1])
    return pairs


def take_rows(pivot_ref, source_ref, out_ref):
    def body(step, carry):
        for i in range(32):
            spot = step * 32 + i
            out_ref[pl.ds(spot, 1), :] = source_ref[pl.ds(pivot_ref[spot], 1), :]
        return carry

    lax.fori_loop(0, K // 32, body, 0)


def choose_kernel(pivot_ref, own_ref, other_ref, chosen_ref, both):
    both[0:K, :] = own_ref[...]
    both[K:, :] = other_ref[...]
    take_rows(pivot_ref, both, chosen_ref)


def choose(pivots, own, other):
    return pl.pallas_call(
        choose_kernel,
        out_shape=jax.ShapeDtypeStruct((K, S), F32),
        in_specs=[smem(), vmem(), vmem()],
        out_specs=vmem(),
        scratch_shapes=[pltpu.VMEM((2 * K, S), F32)],
        compiler_params=params(),
        name="choose",
    )(pivots, own, other)


def eliminate(panel, i):
    lane = lax.broadcasted_iota(jnp.int32, (1, K), 1)
    line = lax.broadcasted_iota(jnp.int32, (BLOCK, K), 0)
    columns = [jnp.broadcast_to(panel[:, i + t : i + t + 1], (BLOCK, K)) for t in range(2)]
    (p, q), (r, s) = [[column[i + t : i + t + 1, :] for column in columns] for t in range(2)]
    rows = [panel[i + t : i + t + 1, :] - jnp.where(lane == i + t, 1.0, 0.0) for t in range(2)]
    scale = 1.0 / (p * s - q * r)
    rows = [(s * rows[0] - q * rows[1]) * scale, (p * rows[1] - r * rows[0]) * scale]
    for t, row in enumerate(rows):
        panel = panel - (columns[t] - jnp.where(line == i + t, 1.0, 0.0)) * row
    return panel


def invert(work):
    count = work.shape[0]
    line = lax.broadcasted_iota(jnp.int32, (BLOCK, K), 0)
    lane = lax.broadcasted_iota(jnp.int32, (BLOCK, K), 1)
    eye = jnp.where(line == lane, 1.0, 0.0)

    def block(step, carry):
        panels = [work[m, 0:BLOCK, :] for m in range(count)]
        before = [panel - eye for panel in panels]
        for i in range(0, BLOCK, 2):
            panels = [eliminate(panel, i) for panel in panels]
        for m in range(count):
            left, right = split3(before[m]), split3(panels[m] - eye)
            pairs = [(0, 0), (0, 1), (1, 0), (1, 1), (0, 2), (2, 0)]
            left = jnp.concatenate([left[i] for i, _ in pairs], axis=0).astype(BF16)
            right = jnp.concatenate([right[j] for _, j in pairs], axis=0).astype(BF16)
            update = lax.dot_general(
                left, right, (((0,), (0,)), ((), ())), preferred_element_type=F32
            )
            turned = pltpu.roll(work[m] - update, K - BLOCK, 1)
            work[m, 0 : K - BLOCK, :] = turned[BLOCK:, :]
            work[m, K - BLOCK : K, :] = turned[:BLOCK, :]
        return carry

    lax.fori_loop(0, K // BLOCK, block, 0)


def dot_rows(left, right):
    return lax.dot_general(
        left,
        right,
        (((1,), (1,)), ((), ())),
        precision=lax.Precision.HIGHEST,
        preferred_element_type=F32,
    )


def scaled_gram(rows):
    eye = lax.broadcasted_iota(jnp.int32, (K, K), 0) == lax.broadcasted_iota(jnp.int32, (K, K), 1)
    gram = dot_rows(rows, rows)
    trace = jnp.sum(jnp.where(eye, gram, 0.0), axis=1, keepdims=True)
    trace = jnp.sum(trace, axis=0, keepdims=True)
    scale = 1.0 / (trace / K + 1e-06)
    return gram * scale + jnp.where(eye, RIDGE, 0.0), scale


def gram_kernel(spot_ref, c0_ref, c1_ref, c2_ref, gram_ref, scale_ref, one_ref, two_ref):
    for level, ref in enumerate((c0_ref, c1_ref, c2_ref)):
        gram_ref[level], scale = scaled_gram(ref[...])
        scale_ref[level] = jnp.broadcast_to(scale, (8, 128))
    one_ref[...] = dot_rows(c0_ref[...], c1_ref[...])
    share = c1_ref[pl.ds(pl.multiple_of(spot_ref[0], 64), 64), :]
    two_ref[...] = dot_rows(share, c2_ref[...])


def tree_kernel(
    pivot_ref, spot_ref, gram_ref, scale_ref, right_one_ref, right_two_ref, c2_ref, o2_ref,
    inverse_ref, one_ref, two_ref, three_ref, root_ref,
    both, c3_ref, work,
):
    both[0:K, :] = c2_ref[...]
    both[K:, :] = o2_ref[...]
    take_rows(pivot_ref, both, c3_ref)
    root_ref[...] = c3_ref[pl.ds(pl.multiple_of(spot_ref[2], 16), 16), :]
    scales = []
    for level in range(3):
        work[level] = gram_ref[level]
        scales.append(scale_ref[level, 0:1, 0:1])
    work[3], scale = scaled_gram(c3_ref[...])
    scales.append(scale)
    invert(work)
    share = c2_ref[pl.ds(pl.multiple_of(spot_ref[1], 32), 32), :]
    rights = (None, right_one_ref[...], right_two_ref[...], dot_rows(share, c3_ref[...]))
    outs = (inverse_ref, one_ref, two_ref, three_ref)
    eye = lax.broadcasted_iota(jnp.int32, (K, K), 0) == lax.broadcasted_iota(jnp.int32, (K, K), 1)
    for level in range(4):
        inverse = (jnp.where(eye, 2.0, 0.0) - work[level]) * scales[level]
        if level > 0:
            inverse = jnp.dot(
                rights[level],
                inverse,
                precision=lax.Precision.HIGHEST,
                preferred_element_type=F32,
            )
        outs[level][...] = inverse


def leaf_kernel(own_ref, a_ref, b_ref, c_ref, c0_ref, inverse_ref, out_ref):
    others = a_ref[...].astype(F32) + b_ref[...].astype(F32) + c_ref[...].astype(F32)
    right = dot_rows(own_ref[...] + others, c0_ref[...])
    out_ref[...] = jnp.dot(
        right, inverse_ref[...], precision=lax.Precision.HIGHEST, preferred_element_type=F32
    )


def body(targets, sources, omega, tree_order, leaf_pivots, pivots_one, pivots_two, pivots_three):
    y, x, z, k = (lax.axis_index(axis) for axis in ALL_AXES)
    leaf = ((y * NX + x) * NZ + z) * NK + k
    bits = (k, z & 1, (z >> 1) & 1)
    tables = (pivots_one, pivots_two, pivots_three)
    pivots = [
        lax.dynamic_index_in_dim(table, leaf >> level + 1, 0, keepdims=False)
        ^ (bits[level] * K).astype(jnp.int32)
        for level, table in enumerate(tables)
    ]

    spots = jnp.stack([k * 64, ((z & 1) * 2 + k) * 32, ((z & 3) * 2 + k) * 16]).astype(jnp.int32)
    ahead = jnp.where(z & 1, 1, -1)
    me = jnp.stack([k] + [(z + d * ahead) & 7 for d in range(4)]).astype(jnp.int32)

    plane = pl.pallas_call(
        pack_kernel,
        out_shape=jax.ShapeDtypeStruct((NZ, 16, 128), F32),
        in_specs=[pl.BlockSpec(memory_space=pltpu.HBM)] * 3,
        out_specs=vmem(),
        scratch_shapes=[
            pltpu.VMEM((2, LEAF), F32),
            pltpu.VMEM((1, LEAF), jnp.int32),
            pltpu.VMEM((1, K), jnp.int32),
            pltpu.SemaphoreType.DMA((3,)),
        ],
        compiler_params=params(),
        name="pack",
    )(targets, tree_order.reshape(1, LEAF), leaf_pivots)
    plane = lax.all_to_all(plane, "z", split_axis=0, concat_axis=0, tiled=True)
    pad = jnp.zeros((14, sources.shape[1]), BF16)
    block = jnp.concatenate([omega, sources, pad], axis=0)
    plane, block, pivots, spots, me = lax.optimization_barrier((plane, block, pivots, spots, me))
    far = lax.ppermute(block, "z", [(s, s ^ 1) for s in range(NZ)])
    weights = [block, swap_cores(block)]
    features = source_features(*weights)
    table = copies_from(plane[:, :8].reshape(NZ * 8, 128), ("y", "x"), NY * NX)
    *leaves, chosen = target_features(me, table, swap_cores(table), plane[:, 8:])
    far, leaves, chosen = lax.optimization_barrier((far, leaves, chosen))
    far = [far, swap_cores(far)]

    def give(part, d):
        return lax.ppermute(part, ZK, along_z(d, True))

    (near,) = sketch_part(chosen, features, weights, [F32], finish=False)
    far_features = source_features(*far)
    c0, *parts = sketch_part(
        chosen, far_features, far, [F32] + [BF16] * 3, start=near
    )
    parts = [give(parts[d - 1], d) for d in (3, 2, 1)]
    weights, features = weights + far, features + far_features
    (third,) = sketch_part(leaves[3], features, weights, [BF16])
    third, parts = lax.optimization_barrier((third, parts))
    third = give(third, 3)
    c0 = c0 + (parts[0].astype(F32) + parts[1].astype(F32) + parts[2].astype(F32))
    c1 = choose(pivots[0], c0, swap_cores(c0))
    c1, leaf = lax.optimization_barrier((c1, leaves[2]))
    other1 = lax.ppermute(c1, "z", [(s, s ^ 1) for s in range(NZ)])
    (second,) = sketch_part(leaf, features, weights, [BF16])
    second, other1 = lax.optimization_barrier((second, other1))
    second = give(second, 2)
    c2 = choose(pivots[1], c1, other1)
    c2, third, leaf = lax.optimization_barrier((c2, third, leaves[1]))
    other2 = lax.ppermute(c2, "z", [(s, s ^ 2) for s in range(NZ)])
    (first,) = sketch_part(leaf, features, weights, [BF16])
    first, leaf = lax.optimization_barrier((first, leaves[0]))
    first = give(first, 1)
    (own,) = sketch_part(leaf, features, weights, [F32])
    own, c0, c1, c2 = lax.optimization_barrier((own, c0, c1, c2))
    grams = pl.pallas_call(
        gram_kernel,
        out_shape=[
            jax.ShapeDtypeStruct((3, K, K), F32),
            jax.ShapeDtypeStruct((3, 8, 128), F32),
            jax.ShapeDtypeStruct((K, K), F32),
            jax.ShapeDtypeStruct((K // 2, K), F32),
        ],
        in_specs=[smem()] + [vmem()] * 3,
        out_specs=[vmem()] * 4,
        compiler_params=params(),
        name="grams",
    )(spots, c0, c1, c2)
    own, second, other2, grams = lax.optimization_barrier((own, second, other2, grams))
    inverse, one_out, two_out, three_out, root = pl.pallas_call(
        tree_kernel,
        out_shape=[
            jax.ShapeDtypeStruct((K, K), F32),
            jax.ShapeDtypeStruct((K, K), F32),
            jax.ShapeDtypeStruct((K // 2, K), F32),
            jax.ShapeDtypeStruct((K // 4, K), F32),
            jax.ShapeDtypeStruct((K // 8, S), F32),
        ],
        in_specs=[smem()] * 2 + [vmem()] * 6,
        out_specs=[vmem()] * 5,
        scratch_shapes=[
            pltpu.VMEM((2 * K, S), F32),
            pltpu.VMEM((K, S), F32),
            pltpu.VMEM((4, K, K), F32),
        ],
        compiler_params=params(),
        name="tree",
    )(pivots[2], spots, *grams, c2, other2)
    leaf_out = pl.pallas_call(
        leaf_kernel,
        out_shape=jax.ShapeDtypeStruct((LEAF, K), F32),
        in_specs=[vmem()] * 6,
        out_specs=vmem(),
        compiler_params=params(),
        name="leaf_interp",
    )(own, third, second, first, c0, inverse)
    return leaf_out, one_out, two_out, three_out, root


def solution(mesh):
    finer = Mesh(mesh.devices.reshape(NY, NX, NZ, NK), ALL_AXES)
    col = ("z", "k")
    placed = (
        P(None, ALL_AXES),
        P(None, col),
        P(None, col),
        P(ALL_AXES),
        P(ALL_AXES, None),
        P(),
        P(),
        P(),
    )
    return jax.shard_map(
        body,
        mesh=finer,
        in_specs=placed,
        out_specs=(P(ALL_AXES, None),) * 5,
        check_vma=False,
    )
```

```python
import functools

import jax
import jax.numpy as jnp
from jax import lax
from jax.experimental import pallas as pl
from jax.experimental.pallas import tpu as pltpu
from jax.sharding import Mesh
from jax.sharding import PartitionSpec as P

LEAF = 512
S = 256
K = 128
FEATURES = 16
BLOCK = 32
RIDGE = 0.1
DELTA_SQUARED = 0.0001
ALL_AXES = ("y", "x", "z", "k")
ZK = ("z", "k")
NY, NX, NZ, NK = 4, 4, 8, 2
F32 = jnp.float32
BF16 = jnp.bfloat16
VMEM_LIMIT = 40 << 20


def params():
    return pltpu.CompilerParams(vmem_limit_bytes=VMEM_LIMIT)


HINT = pl.CostEstimate(flops=1000, transcendentals=0, bytes_accessed=1000)


def smem():
    return pl.BlockSpec(memory_space=pltpu.SMEM)


def vmem():
    return pl.BlockSpec(memory_space=pltpu.VMEM)


def split3(value):
    high = value.astype(BF16).astype(F32)
    rest = value - high
    middle = rest.astype(BF16).astype(F32)
    low = (rest - middle).astype(BF16).astype(F32)
    return high, middle, low


def lookup_kernel(me_ref, own_ref, other_ref, note_ref, *refs):
    outs, chosen_ref, turned = refs[:4], refs[4], refs[5]
    for side, table_ref in enumerate((own_ref, other_ref)):
        for coord in range(2):
            values = jnp.transpose(table_ref[pl.ds(coord, LEAF, stride=2), :])
            for half, part in enumerate(split3(values)[:2]):
                row = (2 * half + coord) * 128
                turned[row : row + 128, side * LEAF : (side + 1) * LEAF] = part.astype(BF16)
    core = me_ref[0]
    line = lax.broadcasted_iota(jnp.int32, (1024, LEAF), 0)
    place = lax.broadcasted_iota(jnp.int32, (128, LEAF), 0)
    spot = lax.broadcasted_iota(jnp.int32, (LEAF, K), 0)
    one = jnp.ones((3, LEAF), F32)
    zero = jnp.zeros((6, LEAF), F32)
    for leaf, out_ref in enumerate(outs):
        note = note_ref[me_ref[1 + leaf]].astype(jnp.int32)
        index = jnp.concatenate([note[i : i + 1, :] for i in range(4)], axis=1)
        row = (((index >> 9) & 1) ^ core) * LEAF + (index >> 10) * 4 + ((index >> 7) & 3)
        hot = jnp.where(line == row, 1.0, 0.0).astype(BF16)
        rows = jnp.dot(turned[...], hot, preferred_element_type=F32)
        rows = rows[:256] + rows[256:]
        mask = place == (index & 127)
        tx = jnp.sum(jnp.where(mask, rows[:128], 0.0), axis=0, keepdims=True)
        ty = jnp.sum(jnp.where(mask, rows[128:], 0.0), axis=0, keepdims=True)
        parts = list(split3(tx)[:2]) + list(split3(ty)[:2])
        parts += list(split3(tx * tx + (ty * ty + DELTA_SQUARED)))
        feature = jnp.concatenate(parts + [one, zero], axis=0)
        out_ref[...] = jnp.transpose(feature).astype(BF16)
        picked = jnp.where(spot == note[4:5, :], 1.0, 0.0).astype(BF16)
        picked = jnp.dot(feature.astype(BF16), picked, preferred_element_type=F32)
        chosen_ref[leaf * K : (leaf + 1) * K, :] = jnp.transpose(picked).astype(BF16)


def pack_kernel(target_hbm, order_hbm, pivot_hbm, out_ref, target_ref, order_ref, pivot_ref, sems):
    pairs = ((target_hbm, target_ref), (order_hbm, order_ref), (pivot_hbm, pivot_ref))
    copies = [
        pltpu.make_async_copy(source, held, sems.at[i]) for i, (source, held) in enumerate(pairs)
    ]
    for copy in copies:
        copy.start()
    for copy in copies:
        copy.wait()
    rows = [
        target_ref[coord : coord + 1, i * 128 : (i + 1) * 128] for i in range(4) for coord in range(2)
    ]
    order = order_ref[...].astype(F32)
    rows += [order[:, i * 128 : (i + 1) * 128] for i in range(4)]
    rows += [pivot_ref[...].astype(F32), jnp.zeros((3, 128), F32)]
    rows = jnp.concatenate(rows, axis=0)
    for i in range(out_ref.shape[0]):
        out_ref[i] = rows


def copies_from(value, axis, size):
    copies = jnp.broadcast_to(value[None], (size, *value.shape))
    parts = lax.all_to_all(copies, axis, split_axis=0, concat_axis=0, tiled=True)
    return parts.reshape(size * value.shape[0], *value.shape[1:])


def target_features(me, own, other, notes):
    return pl.pallas_call(
        lookup_kernel,
        out_shape=[jax.ShapeDtypeStruct((LEAF, FEATURES), BF16)] * 5,
        in_specs=[smem()] + [vmem()] * 3,
        out_specs=[vmem()] * 5,
        scratch_shapes=[pltpu.VMEM((512, 1024), BF16)],
        compiler_params=params(),
        name="lookup",
    )(me, own, other, notes)


def source_kernel(*refs):
    half = len(refs) // 2
    for source_ref, out_ref in zip(refs[:half], refs[half:]):
        points = source_ref[...].astype(F32)
        sx, sy = points[0:1], points[1:2]
        size = split3(sx * sx + sy * sy)
        one = jnp.ones_like(sx)
        zero = jnp.zeros_like(sx)
        rows = [-2.0 * sx] * 2 + [-2.0 * sy] * 2 + [one] * 3 + list(size) + [zero] * 6
        out_ref[...] = jnp.concatenate(rows, axis=0).astype(BF16)


def source_features(*blocks):
    width = blocks[0].shape[1]
    return pl.pallas_call(
        source_kernel,
        grid=(1,),
        out_shape=[jax.ShapeDtypeStruct((FEATURES, width), BF16)] * len(blocks),
        in_specs=[pl.BlockSpec((16, width), lambda i: (S // 16, 0))] * len(blocks),
        out_specs=[pl.BlockSpec((FEATURES, width), lambda i: (0, 0))] * len(blocks),
        compiler_params=params(),
        name="source_features",
    )(*blocks)


def sketch_kernel(target_ref, *refs, blocks, begin, finish, chunk):
    features, weights, refs = refs[:blocks], refs[blocks : 2 * blocks], refs[2 * blocks :]
    start_ref, refs = (None, refs) if begin else (refs[0], refs[1:])
    outs, total_ref = refs[:-1], refs[-1]
    target = target_ref[...]
    width = features[0].shape[1]
    total_ref[...] = jnp.zeros_like(total_ref) if begin else start_ref[...]
    for i in range(blocks):
        total = total_ref[...]
        for j in range(width // chunk):
            span = slice(j * chunk, (j + 1) * chunk)
            squared = jnp.dot(target, features[i][:, span], preferred_element_type=F32)
            panel = jnp.log(squared).astype(BF16)
            total = total + lax.dot_general(
                panel,
                weights[i][0:S, span],
                (((1,), (1,)), ((), ())),
                preferred_element_type=F32,
            )
        if i == blocks - 1:
            total = total * (-0.5) if finish else total
            count = total.shape[0] // len(outs)
            for part, out_ref in enumerate(outs):
                out_ref[...] = total[part * count : (part + 1) * count, :].astype(out_ref.dtype)
        else:
            total_ref[...] = total


def sketch_part(target, features, weights, dtypes, start=None, finish=True):
    count, blocks = target.shape[0], len(weights)
    extra = [] if start is None else [start]
    return pl.pallas_call(
        functools.partial(
            sketch_kernel, blocks=blocks, begin=start is None, finish=finish, chunk=256
        ),
        out_shape=[jax.ShapeDtypeStruct((count // len(dtypes), S), dtype) for dtype in dtypes],
        in_specs=[vmem()] * (1 + 2 * blocks + len(extra)),
        out_specs=[vmem()] * len(dtypes),
        scratch_shapes=[pltpu.VMEM((count, S), F32)],
        cost_estimate=HINT,
        compiler_params=params(),
        name="sketch",
    )(target, *features, *weights, *extra)


def swap_cores(value):
    return lax.ppermute(value, "k", [(0, 1), (1, 0)])


def along_z(step, forward):
    pairs = []
    for sz in range(NZ):
        for sk in range(NK):
            other = (sz + (step if sz % 2 else -step)) % NZ
            pair = (sz * NK + sk, other * NK + sk)
            pairs.append(pair if forward else pair[::-1])
    return pairs


def take_rows(pivot_ref, rows):
    spot = lax.broadcasted_iota(jnp.int32, (rows.shape[0], K), 0)
    hot = jnp.where(spot == pivot_ref[...], 1.0, 0.0).astype(BF16)
    high, middle, low = [
        lax.dot_general(
            hot, part.astype(BF16), (((0,), (0,)), ((), ())), preferred_element_type=F32
        )
        for part in split3(rows)
    ]
    return high + middle + low


def choose_kernel(pivot_ref, own_ref, other_ref, chosen_ref):
    both = jnp.concatenate([own_ref[...], other_ref[...]], axis=0)
    chosen_ref[...] = take_rows(pivot_ref, both)


def choose(pivots, own, other):
    return pl.pallas_call(
        choose_kernel,
        out_shape=jax.ShapeDtypeStruct((K, S), F32),
        in_specs=[vmem()] * 3,
        out_specs=vmem(),
        compiler_params=params(),
        name="choose",
    )(pivots, own, other)


def eliminate(panel, i):
    lane = lax.broadcasted_iota(jnp.int32, (1, K), 1)
    line = lax.broadcasted_iota(jnp.int32, (BLOCK, K), 0)
    columns = [jnp.broadcast_to(panel[:, i + t : i + t + 1], (BLOCK, K)) for t in range(2)]
    (p, q), (r, s) = [[column[i + t : i + t + 1, :] for column in columns] for t in range(2)]
    rows = [panel[i + t : i + t + 1, :] - jnp.where(lane == i + t, 1.0, 0.0) for t in range(2)]
    scale = 1.0 / (p * s - q * r)
    rows = [(s * rows[0] - q * rows[1]) * scale, (p * rows[1] - r * rows[0]) * scale]
    for t, row in enumerate(rows):
        panel = panel - (columns[t] - jnp.where(line == i + t, 1.0, 0.0)) * row
    return panel


def invert(work):
    count = work.shape[0]
    line = lax.broadcasted_iota(jnp.int32, (BLOCK, K), 0)
    lane = lax.broadcasted_iota(jnp.int32, (BLOCK, K), 1)
    eye = jnp.where(line == lane, 1.0, 0.0)

    def block(step, carry):
        panels = [work[m, 0:BLOCK, :] for m in range(count)]
        before = [panel - eye for panel in panels]
        for i in range(0, BLOCK, 2):
            panels = [eliminate(panel, i) for panel in panels]
        for m in range(count):
            left, right = split3(before[m]), split3(panels[m] - eye)
            pairs = [(0, 0), (0, 1), (1, 0), (1, 1), (0, 2), (2, 0)]
            left = jnp.concatenate([left[i] for i, _ in pairs], axis=0).astype(BF16)
            right = jnp.concatenate([right[j] for _, j in pairs], axis=0).astype(BF16)
            update = lax.dot_general(
                left, right, (((0,), (0,)), ((), ())), preferred_element_type=F32
            )
            turned = pltpu.roll(work[m] - update, K - BLOCK, 1)
            work[m, 0 : K - BLOCK, :] = turned[BLOCK:, :]
            work[m, K - BLOCK : K, :] = turned[:BLOCK, :]
        return carry

    lax.fori_loop(0, K // BLOCK, block, 0)


def dot_rows(left, right):
    return lax.dot_general(
        left,
        right,
        (((1,), (1,)), ((), ())),
        precision=lax.Precision.HIGHEST,
        preferred_element_type=F32,
    )


def scaled_gram(rows):
    eye = lax.broadcasted_iota(jnp.int32, (K, K), 0) == lax.broadcasted_iota(jnp.int32, (K, K), 1)
    gram = dot_rows(rows, rows)
    trace = jnp.sum(jnp.where(eye, gram, 0.0), axis=1, keepdims=True)
    trace = jnp.sum(trace, axis=0, keepdims=True)
    scale = 1.0 / (trace / K + 1e-06)
    return gram * scale + jnp.where(eye, RIDGE, 0.0), scale


def gram_kernel(spot_ref, c0_ref, c1_ref, c2_ref, gram_ref, scale_ref, one_ref, two_ref):
    for level, ref in enumerate((c0_ref, c1_ref, c2_ref)):
        gram_ref[level], scale = scaled_gram(ref[...])
        scale_ref[level] = jnp.broadcast_to(scale, (8, 128))
    one_ref[...] = dot_rows(c0_ref[...], c1_ref[...])
    share = c1_ref[pl.ds(pl.multiple_of(spot_ref[0], 64), 64), :]
    two_ref[...] = dot_rows(share, c2_ref[...])


def tree_kernel(
    pivot_ref, spot_ref, gram_ref, scale_ref, right_one_ref, right_two_ref, c2_ref, o2_ref,
    inverse_ref, one_ref, two_ref, three_ref, root_ref,
    c3_ref, work,
):
    c3_ref[...] = take_rows(pivot_ref, jnp.concatenate([c2_ref[...], o2_ref[...]], axis=0))
    root_ref[...] = c3_ref[pl.ds(pl.multiple_of(spot_ref[2], 16), 16), :]
    scales = []
    for level in range(3):
        work[level] = gram_ref[level]
        scales.append(scale_ref[level, 0:1, 0:1])
    work[3], scale = scaled_gram(c3_ref[...])
    scales.append(scale)
    invert(work)
    share = c2_ref[pl.ds(pl.multiple_of(spot_ref[1], 32), 32), :]
    rights = (None, right_one_ref[...], right_two_ref[...], dot_rows(share, c3_ref[...]))
    outs = (inverse_ref, one_ref, two_ref, three_ref)
    eye = lax.broadcasted_iota(jnp.int32, (K, K), 0) == lax.broadcasted_iota(jnp.int32, (K, K), 1)
    for level in range(4):
        inverse = (jnp.where(eye, 2.0, 0.0) - work[level]) * scales[level]
        if level > 0:
            inverse = jnp.dot(
                rights[level],
                inverse,
                precision=lax.Precision.HIGHEST,
                preferred_element_type=F32,
            )
        outs[level][...] = inverse


def leaf_kernel(own_ref, a_ref, b_ref, c_ref, c0_ref, inverse_ref, out_ref):
    others = a_ref[...].astype(F32) + b_ref[...].astype(F32) + c_ref[...].astype(F32)
    right = dot_rows(own_ref[...] + others, c0_ref[...])
    out_ref[...] = jnp.dot(
        right, inverse_ref[...], precision=lax.Precision.HIGHEST, preferred_element_type=F32
    )


def body(targets, sources, omega, tree_order, leaf_pivots, pivots_one, pivots_two, pivots_three):
    y, x, z, k = (lax.axis_index(axis) for axis in ALL_AXES)
    leaf = ((y * NX + x) * NZ + z) * NK + k
    bits = (k, z & 1, (z >> 1) & 1)
    tables = (pivots_one, pivots_two, pivots_three)
    pivots = [
        lax.dynamic_index_in_dim(table, leaf >> level + 1, 0, keepdims=True)
        ^ (bits[level] * K).astype(jnp.int32)
        for level, table in enumerate(tables)
    ]

    spots = jnp.stack([k * 64, ((z & 1) * 2 + k) * 32, ((z & 3) * 2 + k) * 16]).astype(jnp.int32)
    ahead = jnp.where(z & 1, 1, -1)
    me = jnp.stack([k] + [(z + d * ahead) & 7 for d in range(4)]).astype(jnp.int32)

    plane = pl.pallas_call(
        pack_kernel,
        out_shape=jax.ShapeDtypeStruct((NZ, 16, 128), F32),
        in_specs=[pl.BlockSpec(memory_space=pltpu.HBM)] * 3,
        out_specs=vmem(),
        scratch_shapes=[
            pltpu.VMEM((2, LEAF), F32),
            pltpu.VMEM((1, LEAF), jnp.int32),
            pltpu.VMEM((1, K), jnp.int32),
            pltpu.SemaphoreType.DMA((3,)),
        ],
        compiler_params=params(),
        name="pack",
    )(targets, tree_order.reshape(1, LEAF), leaf_pivots)
    plane, omega = lax.optimization_barrier((plane, omega))
    plane = lax.all_to_all(plane, "z", split_axis=0, concat_axis=0, tiled=True)
    pad = jnp.zeros((14, sources.shape[1]), BF16)
    block = jnp.concatenate([omega, sources, pad], axis=0)
    plane, pivots, spots, me = lax.optimization_barrier((plane, pivots, spots, me))
    far = lax.ppermute(block, "z", [(s, s ^ 1) for s in range(NZ)])
    weights = [block, swap_cores(block)]
    features = source_features(*weights)
    table = copies_from(plane[:, :8].reshape(NZ * 8, 128), ("y", "x"), NY * NX)
    *leaves, chosen = target_features(me, table, swap_cores(table), plane[:, 8:])
    far, leaves, chosen = lax.optimization_barrier((far, leaves, chosen))
    far = [far, swap_cores(far)]

    def give(part, d):
        return lax.ppermute(part, ZK, along_z(d, True))

    (near,) = sketch_part(chosen, features, weights, [F32], finish=False)
    far_features = source_features(*far)
    c0, *parts = sketch_part(
        chosen, far_features, far, [F32] + [BF16] * 3, start=near
    )
    parts = [give(parts[d - 1], d) for d in (3, 2, 1)]
    weights, features = weights + far, features + far_features
    (third,) = sketch_part(leaves[3], features, weights, [BF16])
    third, parts = lax.optimization_barrier((third, parts))
    third = give(third, 3)
    c0 = c0 + (parts[0].astype(F32) + parts[1].astype(F32) + parts[2].astype(F32))
    c1 = choose(pivots[0], c0, swap_cores(c0))
    c1, leaf = lax.optimization_barrier((c1, leaves[2]))
    other1 = lax.ppermute(c1, "z", [(s, s ^ 1) for s in range(NZ)])
    (second,) = sketch_part(leaf, features, weights, [BF16])
    second, other1 = lax.optimization_barrier((second, other1))
    second = give(second, 2)
    c2 = choose(pivots[1], c1, other1)
    c2, leaf = lax.optimization_barrier((c2, leaves[1]))
    other2 = lax.ppermute(c2, "z", [(s, s ^ 2) for s in range(NZ)])
    (first,) = sketch_part(leaf, features, weights, [BF16])
    own_leaf, first, third = lax.optimization_barrier((leaves[0], first, third))
    (own,) = sketch_part(own_leaf, features, weights, [F32])
    own, first, other2, c0, c1, c2 = lax.optimization_barrier((own, first, other2, c0, c1, c2))
    first = give(first, 1)
    grams = pl.pallas_call(
        gram_kernel,
        out_shape=[
            jax.ShapeDtypeStruct((3, K, K), F32),
            jax.ShapeDtypeStruct((3, 8, 128), F32),
            jax.ShapeDtypeStruct((K, K), F32),
            jax.ShapeDtypeStruct((K // 2, K), F32),
        ],
        in_specs=[smem()] + [vmem()] * 3,
        out_specs=[vmem()] * 4,
        compiler_params=params(),
        name="grams",
    )(spots, c0, c1, c2)
    second, grams = lax.optimization_barrier((second, grams))
    inverse, one_out, two_out, three_out, root = pl.pallas_call(
        tree_kernel,
        out_shape=[
            jax.ShapeDtypeStruct((K, K), F32),
            jax.ShapeDtypeStruct((K, K), F32),
            jax.ShapeDtypeStruct((K // 2, K), F32),
            jax.ShapeDtypeStruct((K // 4, K), F32),
            jax.ShapeDtypeStruct((K // 8, S), F32),
        ],
        in_specs=[vmem(), smem()] + [vmem()] * 6,
        out_specs=[vmem()] * 5,
        scratch_shapes=[
            pltpu.VMEM((K, S), F32),
            pltpu.VMEM((4, K, K), F32),
        ],
        compiler_params=params(),
        name="tree",
    )(pivots[2], spots, *grams, c2, other2)
    leaf_out = pl.pallas_call(
        leaf_kernel,
        out_shape=jax.ShapeDtypeStruct((LEAF, K), F32),
        in_specs=[vmem()] * 6,
        out_specs=vmem(),
        compiler_params=params(),
        name="leaf_interp",
    )(own, third, second, first, c0, inverse)
    return leaf_out, one_out, two_out, three_out, root


def solution(mesh):
    finer = Mesh(mesh.devices.reshape(NY, NX, NZ, NK), ALL_AXES)
    col = ("z", "k")
    placed = (
        P(None, ALL_AXES),
        P(None, col),
        P(None, col),
        P(ALL_AXES),
        P(ALL_AXES, None),
        P(),
        P(),
        P(),
    )
    return jax.shard_map(
        body,
        mesh=finer,
        in_specs=placed,
        out_specs=(P(ALL_AXES, None),) * 5,
        check_vma=False,
    )
```

```python
import functools

import jax
import jax.numpy as jnp
from jax import lax
from jax.experimental import pallas as pl
from jax.experimental.pallas import tpu as pltpu
from jax.sharding import Mesh
from jax.sharding import PartitionSpec as P

LEAF = 512
S = 256
K = 128
FEATURES = 16
BLOCK = 32
RIDGE = 0.1
DELTA_SQUARED = 0.0001
ALL_AXES = ("y", "x", "z", "k")
ZK = ("z", "k")
NY, NX, NZ, NK = 4, 4, 8, 2
F32 = jnp.float32
BF16 = jnp.bfloat16
VMEM_LIMIT = 40 << 20


def params():
    return pltpu.CompilerParams(vmem_limit_bytes=VMEM_LIMIT)


HINT = pl.CostEstimate(flops=1000, transcendentals=0, bytes_accessed=1000)


def smem():
    return pl.BlockSpec(memory_space=pltpu.SMEM)


def vmem():
    return pl.BlockSpec(memory_space=pltpu.VMEM)


def split3(value):
    high = value.astype(BF16).astype(F32)
    rest = value - high
    middle = rest.astype(BF16).astype(F32)
    low = (rest - middle).astype(BF16).astype(F32)
    return high, middle, low


def lookup_kernel(me_ref, own_ref, other_ref, note_ref, *refs):
    outs, chosen_ref, turned = refs[:4], refs[4], refs[5]
    for side, table_ref in enumerate((own_ref, other_ref)):
        for coord in range(2):
            values = jnp.transpose(table_ref[pl.ds(coord, LEAF, stride=2), :])
            for half, part in enumerate(split3(values)[:2]):
                row = (2 * half + coord) * 128
                turned[row : row + 128, side * LEAF : (side + 1) * LEAF] = part.astype(BF16)
    core = me_ref[0]
    line = lax.broadcasted_iota(jnp.int32, (1024, LEAF), 0)
    place = lax.broadcasted_iota(jnp.int32, (128, LEAF), 0)
    spot = lax.broadcasted_iota(jnp.int32, (LEAF, K), 0)
    one = jnp.ones((3, LEAF), F32)
    zero = jnp.zeros((6, LEAF), F32)
    for leaf, out_ref in enumerate(outs):
        note = note_ref[me_ref[1 + leaf]].astype(jnp.int32)
        index = jnp.concatenate([note[i : i + 1, :] for i in range(4)], axis=1)
        row = (((index >> 9) & 1) ^ core) * LEAF + (index >> 10) * 4 + ((index >> 7) & 3)
        hot = jnp.where(line == row, 1.0, 0.0).astype(BF16)
        rows = jnp.dot(turned[...], hot, preferred_element_type=F32)
        rows = rows[:256] + rows[256:]
        mask = place == (index & 127)
        tx = jnp.sum(jnp.where(mask, rows[:128], 0.0), axis=0, keepdims=True)
        ty = jnp.sum(jnp.where(mask, rows[128:], 0.0), axis=0, keepdims=True)
        parts = list(split3(tx)[:2]) + list(split3(ty)[:2])
        parts += list(split3(tx * tx + (ty * ty + DELTA_SQUARED)))
        feature = jnp.concatenate(parts + [one, zero], axis=0)
        out_ref[...] = jnp.transpose(feature).astype(BF16)
        picked = jnp.where(spot == note[4:5, :], 1.0, 0.0).astype(BF16)
        picked = jnp.dot(feature.astype(BF16), picked, preferred_element_type=F32)
        chosen_ref[leaf * K : (leaf + 1) * K, :] = jnp.transpose(picked).astype(BF16)


def in_hbm(value):
    return pltpu.with_memory_space_constraint(value, pltpu.HBM)


def pack_kernel(target_hbm, order_hbm, pivot_hbm, out_ref, target_ref, order_ref, pivot_ref, sems):
    pairs = ((target_hbm, target_ref), (order_hbm, order_ref), (pivot_hbm, pivot_ref))
    copies = [
        pltpu.make_async_copy(source, held, sems.at[i]) for i, (source, held) in enumerate(pairs)
    ]
    for copy in copies:
        copy.start()
    for copy in copies:
        copy.wait()
    rows = [
        target_ref[coord : coord + 1, i * 128 : (i + 1) * 128] for i in range(4) for coord in range(2)
    ]
    order = order_ref[...].astype(F32)
    rows += [order[:, i * 128 : (i + 1) * 128] for i in range(4)]
    rows += [pivot_ref[...].astype(F32), jnp.zeros((3, 128), F32)]
    rows = jnp.concatenate(rows, axis=0)
    for i in range(out_ref.shape[0]):
        out_ref[i] = rows


def copies_from(value, axis, size):
    copies = jnp.broadcast_to(value[None], (size, *value.shape))
    parts = lax.all_to_all(copies, axis, split_axis=0, concat_axis=0, tiled=True)
    return parts.reshape(size * value.shape[0], *value.shape[1:])


def target_features(me, own, other, notes):
    return pl.pallas_call(
        lookup_kernel,
        out_shape=[jax.ShapeDtypeStruct((LEAF, FEATURES), BF16)] * 5,
        in_specs=[smem()] + [vmem()] * 3,
        out_specs=[vmem()] * 5,
        scratch_shapes=[pltpu.VMEM((512, 1024), BF16)],
        compiler_params=params(),
        name="lookup",
    )(me, own, other, notes)


def source_kernel(*refs):
    half = len(refs) // 2
    for source_ref, out_ref in zip(refs[:half], refs[half:]):
        points = source_ref[...].astype(F32)
        sx, sy = points[0:1], points[1:2]
        size = split3(sx * sx + sy * sy)
        one = jnp.ones_like(sx)
        zero = jnp.zeros_like(sx)
        rows = [-2.0 * sx] * 2 + [-2.0 * sy] * 2 + [one] * 3 + list(size) + [zero] * 6
        out_ref[...] = jnp.concatenate(rows, axis=0).astype(BF16)


def source_features(*blocks):
    width = blocks[0].shape[1]
    return pl.pallas_call(
        source_kernel,
        grid=(1,),
        out_shape=[jax.ShapeDtypeStruct((FEATURES, width), BF16)] * len(blocks),
        in_specs=[pl.BlockSpec((16, width), lambda i: (S // 16, 0))] * len(blocks),
        out_specs=[pl.BlockSpec((FEATURES, width), lambda i: (0, 0))] * len(blocks),
        compiler_params=params(),
        name="source_features",
    )(*blocks)


def sketch_kernel(target_ref, *refs, blocks, begin, finish, chunk):
    features, weights, refs = refs[:blocks], refs[blocks : 2 * blocks], refs[2 * blocks :]
    start_ref, refs = (None, refs) if begin else (refs[0], refs[1:])
    outs, total_ref = refs[:-1], refs[-1]
    target = target_ref[...]
    width = features[0].shape[1]
    total_ref[...] = jnp.zeros_like(total_ref) if begin else start_ref[...]
    for i in range(blocks):
        total = total_ref[...]
        for j in range(width // chunk):
            span = slice(j * chunk, (j + 1) * chunk)
            squared = jnp.dot(target, features[i][:, span], preferred_element_type=F32)
            panel = jnp.log(squared).astype(BF16)
            total = total + lax.dot_general(
                panel,
                weights[i][0:S, span],
                (((1,), (1,)), ((), ())),
                preferred_element_type=F32,
            )
        if i == blocks - 1:
            total = total * (-0.5) if finish else total
            count = total.shape[0] // len(outs)
            for part, out_ref in enumerate(outs):
                out_ref[...] = total[part * count : (part + 1) * count, :].astype(out_ref.dtype)
        else:
            total_ref[...] = total


def sketch_part(target, features, weights, dtypes, start=None, finish=True):
    count, blocks = target.shape[0], len(weights)
    extra = [] if start is None else [start]
    return pl.pallas_call(
        functools.partial(
            sketch_kernel, blocks=blocks, begin=start is None, finish=finish, chunk=256
        ),
        out_shape=[jax.ShapeDtypeStruct((count // len(dtypes), S), dtype) for dtype in dtypes],
        in_specs=[vmem()] * (1 + 2 * blocks + len(extra)),
        out_specs=[vmem()] * len(dtypes),
        scratch_shapes=[pltpu.VMEM((count, S), F32)],
        cost_estimate=HINT,
        compiler_params=params(),
        name="sketch",
    )(target, *features, *weights, *extra)


def swap_cores(value):
    return lax.ppermute(value, "k", [(0, 1), (1, 0)])


def along_z(step, forward):
    pairs = []
    for sz in range(NZ):
        for sk in range(NK):
            other = (sz + (step if sz % 2 else -step)) % NZ
            pair = (sz * NK + sk, other * NK + sk)
            pairs.append(pair if forward else pair[::-1])
    return pairs


def take_rows(pivots, rows):
    spot = lax.broadcasted_iota(jnp.int32, (rows.shape[0], K), 0)
    hot = jnp.where(spot == pivots, 1.0, 0.0).astype(BF16)
    high, middle, low = [
        lax.dot_general(
            hot, part.astype(BF16), (((0,), (0,)), ((), ())), preferred_element_type=F32
        )
        for part in split3(rows)
    ]
    return high + middle + low


def choose_kernel(spot_ref, table_ref, own_ref, other_ref, chosen_ref, *, level):
    both = jnp.concatenate([own_ref[...], other_ref[...]], axis=0)
    chosen_ref[...] = take_rows(node_pivots(spot_ref, table_ref, level), both)


def node_pivots(spot_ref, table_ref, level):
    return table_ref[pl.ds(spot_ref[3 + level], 1), :] ^ spot_ref[6 + level]


def choose(level, spots, table, own, other):
    return pl.pallas_call(
        functools.partial(choose_kernel, level=level),
        out_shape=jax.ShapeDtypeStruct((K, S), F32),
        in_specs=[smem()] + [vmem()] * 3,
        out_specs=vmem(),
        compiler_params=params(),
        name="choose",
    )(spots, table, own, other)


def eliminate(panel, i):
    lane = lax.broadcasted_iota(jnp.int32, (1, K), 1)
    line = lax.broadcasted_iota(jnp.int32, (BLOCK, K), 0)
    columns = [jnp.broadcast_to(panel[:, i + t : i + t + 1], (BLOCK, K)) for t in range(2)]
    (p, q), (r, s) = [[column[i + t : i + t + 1, :] for column in columns] for t in range(2)]
    rows = [panel[i + t : i + t + 1, :] - jnp.where(lane == i + t, 1.0, 0.0) for t in range(2)]
    scale = 1.0 / (p * s - q * r)
    rows = [(s * rows[0] - q * rows[1]) * scale, (p * rows[1] - r * rows[0]) * scale]
    for t, row in enumerate(rows):
        panel = panel - (columns[t] - jnp.where(line == i + t, 1.0, 0.0)) * row
    return panel


def invert(work):
    count = work.shape[0]
    line = lax.broadcasted_iota(jnp.int32, (BLOCK, K), 0)
    lane = lax.broadcasted_iota(jnp.int32, (BLOCK, K), 1)
    eye = jnp.where(line == lane, 1.0, 0.0)

    def block(step, carry):
        panels = [work[m, 0:BLOCK, :] for m in range(count)]
        before = [panel - eye for panel in panels]
        for i in range(0, BLOCK, 2):
            panels = [eliminate(panel, i) for panel in panels]
        for m in range(count):
            left, right = split3(before[m]), split3(panels[m] - eye)
            pairs = [(0, 0), (0, 1), (1, 0), (1, 1), (0, 2), (2, 0)]
            left = jnp.concatenate([left[i] for i, _ in pairs], axis=0).astype(BF16)
            right = jnp.concatenate([right[j] for _, j in pairs], axis=0).astype(BF16)
            update = lax.dot_general(
                left, right, (((0,), (0,)), ((), ())), preferred_element_type=F32
            )
            turned = pltpu.roll(work[m] - update, K - BLOCK, 1)
            work[m, 0 : K - BLOCK, :] = turned[BLOCK:, :]
            work[m, K - BLOCK : K, :] = turned[:BLOCK, :]
        return carry

    lax.fori_loop(0, K // BLOCK, block, 0)


def dot_rows(left, right):
    return lax.dot_general(
        left,
        right,
        (((1,), (1,)), ((), ())),
        precision=lax.Precision.HIGHEST,
        preferred_element_type=F32,
    )


def scaled_gram(rows):
    eye = lax.broadcasted_iota(jnp.int32, (K, K), 0) == lax.broadcasted_iota(jnp.int32, (K, K), 1)
    gram = dot_rows(rows, rows)
    trace = jnp.sum(jnp.where(eye, gram, 0.0), axis=1, keepdims=True)
    trace = jnp.sum(trace, axis=0, keepdims=True)
    scale = 1.0 / (trace / K + 1e-06)
    return gram * scale + jnp.where(eye, RIDGE, 0.0), scale


def gram_kernel(spot_ref, c0_ref, c1_ref, c2_ref, gram_ref, scale_ref, one_ref, two_ref):
    for level, ref in enumerate((c0_ref, c1_ref, c2_ref)):
        gram_ref[level], scale = scaled_gram(ref[...])
        scale_ref[level] = jnp.broadcast_to(scale, (8, 128))
    one_ref[...] = dot_rows(c0_ref[...], c1_ref[...])
    share = c1_ref[pl.ds(pl.multiple_of(spot_ref[0], 64), 64), :]
    two_ref[...] = dot_rows(share, c2_ref[...])


def tree_kernel(
    table_ref, spot_ref, gram_ref, scale_ref, right_one_ref, right_two_ref, c2_ref, o2_ref,
    inverse_ref, one_ref, two_ref, three_ref, root_ref,
    c3_ref, work,
):
    both = jnp.concatenate([c2_ref[...], o2_ref[...]], axis=0)
    c3_ref[...] = take_rows(node_pivots(spot_ref, table_ref, 2), both)
    root_ref[...] = c3_ref[pl.ds(pl.multiple_of(spot_ref[2], 16), 16), :]
    scales = []
    for level in range(3):
        work[level] = gram_ref[level]
        scales.append(scale_ref[level, 0:1, 0:1])
    work[3], scale = scaled_gram(c3_ref[...])
    scales.append(scale)
    invert(work)
    share = c2_ref[pl.ds(pl.multiple_of(spot_ref[1], 32), 32), :]
    rights = (None, right_one_ref[...], right_two_ref[...], dot_rows(share, c3_ref[...]))
    outs = (inverse_ref, one_ref, two_ref, three_ref)
    eye = lax.broadcasted_iota(jnp.int32, (K, K), 0) == lax.broadcasted_iota(jnp.int32, (K, K), 1)
    for level in range(4):
        inverse = (jnp.where(eye, 2.0, 0.0) - work[level]) * scales[level]
        if level > 0:
            inverse = jnp.dot(
                rights[level],
                inverse,
                precision=lax.Precision.HIGHEST,
                preferred_element_type=F32,
            )
        outs[level][...] = inverse


def leaf_kernel(own_ref, a_ref, b_ref, c_ref, c0_ref, inverse_ref, out_ref):
    others = a_ref[...].astype(F32) + b_ref[...].astype(F32) + c_ref[...].astype(F32)
    right = dot_rows(own_ref[...] + others, c0_ref[...])
    out_ref[...] = jnp.dot(
        right, inverse_ref[...], precision=lax.Precision.HIGHEST, preferred_element_type=F32
    )


def body(targets, sources, omega, tree_order, leaf_pivots, pivots_one, pivots_two, pivots_three):
    y, x, z, k = (lax.axis_index(axis) for axis in ALL_AXES)
    leaf = ((y * NX + x) * NZ + z) * NK + k
    spots = [k * 64, ((z & 1) * 2 + k) * 32, ((z & 3) * 2 + k) * 16]
    spots += [leaf >> level + 1 for level in range(3)]
    spots += [bit * K for bit in (k, z & 1, (z >> 1) & 1)]
    spots = jnp.stack(spots).astype(jnp.int32)
    ahead = jnp.where(z & 1, 1, -1)
    me = jnp.stack([k] + [(z + d * ahead) & 7 for d in range(4)]).astype(jnp.int32)

    plane = pl.pallas_call(
        pack_kernel,
        out_shape=jax.ShapeDtypeStruct((NZ, 16, 128), F32),
        in_specs=[pl.BlockSpec(memory_space=pltpu.HBM)] * 3,
        out_specs=vmem(),
        scratch_shapes=[
            pltpu.VMEM((2, LEAF), F32),
            pltpu.VMEM((1, LEAF), jnp.int32),
            pltpu.VMEM((1, K), jnp.int32),
            pltpu.SemaphoreType.DMA((3,)),
        ],
        compiler_params=params(),
        name="pack",
    )(*(in_hbm(part) for part in (targets, tree_order.reshape(1, LEAF), leaf_pivots)))
    plane, omega = lax.optimization_barrier((plane, omega))
    plane = lax.all_to_all(plane, "z", split_axis=0, concat_axis=0, tiled=True)
    pad = jnp.zeros((14, sources.shape[1]), BF16)
    block = jnp.concatenate([omega, sources, pad], axis=0)
    plane, spots, me = lax.optimization_barrier((plane, spots, me))
    far = lax.ppermute(block, "z", [(s, s ^ 1) for s in range(NZ)])
    weights = [block, swap_cores(block)]
    features = source_features(*weights)
    table = copies_from(plane[:, :8].reshape(NZ * 8, 128), ("y", "x"), NY * NX)
    *leaves, chosen = target_features(me, table, swap_cores(table), plane[:, 8:])
    far, leaves, chosen = lax.optimization_barrier((far, leaves, chosen))
    far = [far, swap_cores(far)]

    def give(part, d):
        return lax.ppermute(part, ZK, along_z(d, True))

    (near,) = sketch_part(chosen, features, weights, [F32], finish=False)
    far_features = source_features(*far)
    c0, *parts = sketch_part(
        chosen, far_features, far, [F32] + [BF16] * 3, start=near
    )
    parts = [give(parts[d - 1], d) for d in (3, 2, 1)]
    weights, features = weights + far, features + far_features
    (third,) = sketch_part(leaves[3], features, weights, [BF16])
    third, parts = lax.optimization_barrier((third, parts))
    third = give(third, 3)
    c0 = c0 + (parts[0].astype(F32) + parts[1].astype(F32) + parts[2].astype(F32))
    c1 = choose(0, spots, pivots_one, c0, swap_cores(c0))
    c1, leaf = lax.optimization_barrier((c1, leaves[2]))
    other1 = lax.ppermute(c1, "z", [(s, s ^ 1) for s in range(NZ)])
    (second,) = sketch_part(leaf, features, weights, [BF16])
    second, other1 = lax.optimization_barrier((second, other1))
    second = give(second, 2)
    c2 = choose(1, spots, pivots_two, c1, other1)
    c2, leaf = lax.optimization_barrier((c2, leaves[1]))
    other2 = lax.ppermute(c2, "z", [(s, s ^ 2) for s in range(NZ)])
    (first,) = sketch_part(leaf, features, weights, [BF16])
    own_leaf, first, third = lax.optimization_barrier((leaves[0], first, third))
    (own,) = sketch_part(own_leaf, features, weights, [F32])
    own, first, other2, c0, c1, c2 = lax.optimization_barrier((own, first, other2, c0, c1, c2))
    first = give(first, 1)
    grams = pl.pallas_call(
        gram_kernel,
        out_shape=[
            jax.ShapeDtypeStruct((3, K, K), F32),
            jax.ShapeDtypeStruct((3, 8, 128), F32),
            jax.ShapeDtypeStruct((K, K), F32),
            jax.ShapeDtypeStruct((K // 2, K), F32),
        ],
        in_specs=[smem()] + [vmem()] * 3,
        out_specs=[vmem()] * 4,
        compiler_params=params(),
        name="grams",
    )(spots, c0, c1, c2)
    second, grams = lax.optimization_barrier((second, grams))
    inverse, one_out, two_out, three_out, root = pl.pallas_call(
        tree_kernel,
        out_shape=[
            jax.ShapeDtypeStruct((K, K), F32),
            jax.ShapeDtypeStruct((K, K), F32),
            jax.ShapeDtypeStruct((K // 2, K), F32),
            jax.ShapeDtypeStruct((K // 4, K), F32),
            jax.ShapeDtypeStruct((K // 8, S), F32),
        ],
        in_specs=[vmem(), smem()] + [vmem()] * 6,
        out_specs=[vmem()] * 5,
        scratch_shapes=[
            pltpu.VMEM((K, S), F32),
            pltpu.VMEM((4, K, K), F32),
        ],
        compiler_params=params(),
        name="tree",
    )(pivots_three, spots, *grams, c2, other2)
    leaf_out = pl.pallas_call(
        leaf_kernel,
        out_shape=jax.ShapeDtypeStruct((LEAF, K), F32),
        in_specs=[vmem()] * 6,
        out_specs=vmem(),
        compiler_params=params(),
        name="leaf_interp",
    )(own, third, second, first, c0, inverse)
    return leaf_out, one_out, two_out, three_out, root


def solution(mesh):
    finer = Mesh(mesh.devices.reshape(NY, NX, NZ, NK), ALL_AXES)
    col = ("z", "k")
    placed = (
        P(None, ALL_AXES),
        P(None, col),
        P(None, col),
        P(ALL_AXES),
        P(ALL_AXES, None),
        P(),
        P(),
        P(),
    )
    return jax.shard_map(
        body,
        mesh=finer,
        in_specs=placed,
        out_specs=(P(ALL_AXES, None),) * 5,
        check_vma=False,
    )
```

```python
import functools

import jax
import jax.numpy as jnp
from jax import lax
from jax.experimental import pallas as pl
from jax.experimental.pallas import tpu as pltpu
from jax.sharding import Mesh
from jax.sharding import PartitionSpec as P

LEAF = 512
S = 256
K = 128
FEATURES = 16
BLOCK = 32
RIDGE = 0.1
DELTA_SQUARED = 0.0001
ALL_AXES = ("y", "x", "z", "k")
ZK = ("z", "k")
NY, NX, NZ, NK = 4, 4, 8, 2
F32 = jnp.float32
BF16 = jnp.bfloat16
VMEM_LIMIT = 40 << 20


def params():
    return pltpu.CompilerParams(vmem_limit_bytes=VMEM_LIMIT)


HINT = pl.CostEstimate(flops=1000, transcendentals=0, bytes_accessed=1000)


def smem():
    return pl.BlockSpec(memory_space=pltpu.SMEM)


def vmem():
    return pl.BlockSpec(memory_space=pltpu.VMEM)


def split3(value):
    high = value.astype(BF16).astype(F32)
    rest = value - high
    middle = rest.astype(BF16).astype(F32)
    low = (rest - middle).astype(BF16).astype(F32)
    return high, middle, low


def lookup_kernel(me_ref, own_ref, other_ref, note_ref, *refs):
    outs, chosen_ref, turned = refs[:4], refs[4], refs[5]
    for side, table_ref in enumerate((own_ref, other_ref)):
        for coord in range(2):
            values = jnp.transpose(table_ref[pl.ds(coord, LEAF, stride=2), :])
            for half, part in enumerate(split3(values)[:2]):
                row = (2 * half + coord) * 128
                turned[row : row + 128, side * LEAF : (side + 1) * LEAF] = part.astype(BF16)
    core = me_ref[0]
    line = lax.broadcasted_iota(jnp.int32, (1024, LEAF), 0)
    place = lax.broadcasted_iota(jnp.int32, (128, LEAF), 0)
    spot = lax.broadcasted_iota(jnp.int32, (LEAF, K), 0)
    one = jnp.ones((3, LEAF), F32)
    zero = jnp.zeros((6, LEAF), F32)
    for leaf, out_ref in enumerate(outs):
        note = note_ref[me_ref[1 + leaf]].astype(jnp.int32)
        index = jnp.concatenate([note[i : i + 1, :] for i in range(4)], axis=1)
        row = (((index >> 9) & 1) ^ core) * LEAF + (index >> 10) * 4 + ((index >> 7) & 3)
        hot = jnp.where(line == row, 1.0, 0.0).astype(BF16)
        rows = jnp.dot(turned[...], hot, preferred_element_type=F32)
        rows = rows[:256] + rows[256:]
        mask = place == (index & 127)
        tx = jnp.sum(jnp.where(mask, rows[:128], 0.0), axis=0, keepdims=True)
        ty = jnp.sum(jnp.where(mask, rows[128:], 0.0), axis=0, keepdims=True)
        parts = list(split3(tx)[:2]) + list(split3(ty)[:2])
        parts += list(split3(tx * tx + (ty * ty + DELTA_SQUARED)))
        feature = jnp.concatenate(parts + [one, zero], axis=0)
        out_ref[...] = jnp.transpose(feature).astype(BF16)
        picked = jnp.where(spot == note[4:5, :], 1.0, 0.0).astype(BF16)
        picked = jnp.dot(feature.astype(BF16), picked, preferred_element_type=F32)
        chosen_ref[leaf * K : (leaf + 1) * K, :] = jnp.transpose(picked).astype(BF16)


def in_hbm(value):
    return pltpu.with_memory_space_constraint(value, pltpu.HBM)


def pack_kernel(target_hbm, order_hbm, pivot_hbm, out_ref, target_ref, order_ref, pivot_ref, sems):
    pairs = ((target_hbm, target_ref), (order_hbm, order_ref), (pivot_hbm, pivot_ref))
    copies = [
        pltpu.make_async_copy(source, held, sems.at[i]) for i, (source, held) in enumerate(pairs)
    ]
    for copy in copies:
        copy.start()
    for copy in copies:
        copy.wait()
    rows = [
        target_ref[coord : coord + 1, i * 128 : (i + 1) * 128] for i in range(4) for coord in range(2)
    ]
    order = order_ref[...].astype(F32)
    rows += [order[:, i * 128 : (i + 1) * 128] for i in range(4)]
    rows += [pivot_ref[...].astype(F32), jnp.zeros((3, 128), F32)]
    rows = jnp.concatenate(rows, axis=0)
    for i in range(out_ref.shape[0]):
        out_ref[i] = rows


def copies_from(value, axis, size):
    copies = jnp.broadcast_to(value[None], (size, *value.shape))
    parts = lax.all_to_all(copies, axis, split_axis=0, concat_axis=0, tiled=True)
    return parts.reshape(size * value.shape[0], *value.shape[1:])


def target_features(me, own, other, notes):
    return pl.pallas_call(
        lookup_kernel,
        out_shape=[jax.ShapeDtypeStruct((LEAF, FEATURES), BF16)] * 5,
        in_specs=[smem()] + [vmem()] * 3,
        out_specs=[vmem()] * 5,
        scratch_shapes=[pltpu.VMEM((512, 1024), BF16)],
        compiler_params=params(),
        name="lookup",
    )(me, own, other, notes)


def source_kernel(*refs):
    half = len(refs) // 2
    for source_ref, out_ref in zip(refs[:half], refs[half:]):
        points = source_ref[...].astype(F32)
        sx, sy = points[0:1], points[1:2]
        size = split3(sx * sx + sy * sy)
        one = jnp.ones_like(sx)
        zero = jnp.zeros_like(sx)
        rows = [-2.0 * sx] * 2 + [-2.0 * sy] * 2 + [one] * 3 + list(size) + [zero] * 6
        out_ref[...] = jnp.concatenate(rows, axis=0).astype(BF16)


def source_features(*blocks):
    width = blocks[0].shape[1]
    return pl.pallas_call(
        source_kernel,
        grid=(1,),
        out_shape=[jax.ShapeDtypeStruct((FEATURES, width), BF16)] * len(blocks),
        in_specs=[pl.BlockSpec((16, width), lambda i: (S // 16, 0))] * len(blocks),
        out_specs=[pl.BlockSpec((FEATURES, width), lambda i: (0, 0))] * len(blocks),
        compiler_params=params(),
        name="source_features",
    )(*blocks)


def sketch_kernel(target_ref, *refs, blocks, begin, finish, chunk):
    features, weights, refs = refs[:blocks], refs[blocks : 2 * blocks], refs[2 * blocks :]
    start_ref, refs = (None, refs) if begin else (refs[0], refs[1:])
    outs, total_ref = refs[:-1], refs[-1]
    target = target_ref[...]
    width = features[0].shape[1]
    total_ref[...] = jnp.zeros_like(total_ref) if begin else start_ref[...]
    for i in range(blocks):
        total = total_ref[...]
        for j in range(width // chunk):
            span = slice(j * chunk, (j + 1) * chunk)
            squared = jnp.dot(target, features[i][:, span], preferred_element_type=F32)
            panel = jnp.log(squared).astype(BF16)
            total = total + lax.dot_general(
                panel,
                weights[i][0:S, span],
                (((1,), (1,)), ((), ())),
                preferred_element_type=F32,
            )
        if i == blocks - 1:
            total = total * (-0.5) if finish else total
            count = total.shape[0] // len(outs)
            for part, out_ref in enumerate(outs):
                out_ref[...] = total[part * count : (part + 1) * count, :].astype(out_ref.dtype)
        else:
            total_ref[...] = total


def sketch_part(target, features, weights, dtypes, start=None, finish=True):
    count, blocks = target.shape[0], len(weights)
    extra = [] if start is None else [start]
    return pl.pallas_call(
        functools.partial(
            sketch_kernel, blocks=blocks, begin=start is None, finish=finish, chunk=256
        ),
        out_shape=[jax.ShapeDtypeStruct((count // len(dtypes), S), dtype) for dtype in dtypes],
        in_specs=[vmem()] * (1 + 2 * blocks + len(extra)),
        out_specs=[vmem()] * len(dtypes),
        scratch_shapes=[pltpu.VMEM((count, S), F32)],
        cost_estimate=HINT,
        compiler_params=params(),
        name="sketch",
    )(target, *features, *weights, *extra)


def swap_cores(value):
    return lax.ppermute(value, "k", [(0, 1), (1, 0)])


def along_z(step, forward):
    pairs = []
    for sz in range(NZ):
        for sk in range(NK):
            other = (sz + (step if sz % 2 else -step)) % NZ
            pair = (sz * NK + sk, other * NK + sk)
            pairs.append(pair if forward else pair[::-1])
    return pairs


def take_rows(pivots, rows):
    spot = lax.broadcasted_iota(jnp.int32, (rows.shape[0], K), 0)
    hot = jnp.where(spot == pivots, 1.0, 0.0).astype(BF16)
    high, middle, low = [
        lax.dot_general(
            hot, part.astype(BF16), (((0,), (0,)), ((), ())), preferred_element_type=F32
        )
        for part in split3(rows)
    ]
    return high + middle + low


def choose_kernel(pivot_ref, own_ref, other_ref, chosen_ref):
    both = jnp.concatenate([own_ref[...], other_ref[...]], axis=0)
    chosen_ref[...] = take_rows(pivot_ref[...], both)


def choose(pivots, own, other):
    return pl.pallas_call(
        choose_kernel,
        out_shape=jax.ShapeDtypeStruct((K, S), F32),
        in_specs=[vmem()] * 3,
        out_specs=vmem(),
        compiler_params=params(),
        name="choose",
    )(pivots, own, other)


def eliminate(panel, i):
    lane = lax.broadcasted_iota(jnp.int32, (1, K), 1)
    line = lax.broadcasted_iota(jnp.int32, (BLOCK, K), 0)
    columns = [jnp.broadcast_to(panel[:, i + t : i + t + 1], (BLOCK, K)) for t in range(2)]
    (p, q), (r, s) = [[column[i + t : i + t + 1, :] for column in columns] for t in range(2)]
    rows = [panel[i + t : i + t + 1, :] - jnp.where(lane == i + t, 1.0, 0.0) for t in range(2)]
    scale = 1.0 / (p * s - q * r)
    rows = [(s * rows[0] - q * rows[1]) * scale, (p * rows[1] - r * rows[0]) * scale]
    for t, row in enumerate(rows):
        panel = panel - (columns[t] - jnp.where(line == i + t, 1.0, 0.0)) * row
    return panel


def invert(work):
    count = work.shape[0]
    line = lax.broadcasted_iota(jnp.int32, (BLOCK, K), 0)
    lane = lax.broadcasted_iota(jnp.int32, (BLOCK, K), 1)
    eye = jnp.where(line == lane, 1.0, 0.0)

    def block(step, carry):
        panels = [work[m, 0:BLOCK, :] for m in range(count)]
        before = [panel - eye for panel in panels]
        for i in range(0, BLOCK, 2):
            panels = [eliminate(panel, i) for panel in panels]
        for m in range(count):
            left, right = split3(before[m]), split3(panels[m] - eye)
            pairs = [(0, 0), (0, 1), (1, 0), (1, 1), (0, 2), (2, 0)]
            left = jnp.concatenate([left[i] for i, _ in pairs], axis=0).astype(BF16)
            right = jnp.concatenate([right[j] for _, j in pairs], axis=0).astype(BF16)
            update = lax.dot_general(
                left, right, (((0,), (0,)), ((), ())), preferred_element_type=F32
            )
            turned = pltpu.roll(work[m] - update, K - BLOCK, 1)
            work[m, 0 : K - BLOCK, :] = turned[BLOCK:, :]
            work[m, K - BLOCK : K, :] = turned[:BLOCK, :]
        return carry

    lax.fori_loop(0, K // BLOCK, block, 0)


def dot_rows(left, right):
    return lax.dot_general(
        left,
        right,
        (((1,), (1,)), ((), ())),
        precision=lax.Precision.HIGHEST,
        preferred_element_type=F32,
    )


def scaled_gram(rows):
    eye = lax.broadcasted_iota(jnp.int32, (K, K), 0) == lax.broadcasted_iota(jnp.int32, (K, K), 1)
    gram = dot_rows(rows, rows)
    trace = jnp.sum(jnp.where(eye, gram, 0.0), axis=1, keepdims=True)
    trace = jnp.sum(trace, axis=0, keepdims=True)
    scale = 1.0 / (trace / K + 1e-06)
    return gram * scale + jnp.where(eye, RIDGE, 0.0), scale


def gram_kernel(spot_ref, c0_ref, c1_ref, c2_ref, gram_ref, scale_ref, one_ref, two_ref):
    for level, ref in enumerate((c0_ref, c1_ref, c2_ref)):
        gram_ref[level], scale = scaled_gram(ref[...])
        scale_ref[level] = jnp.broadcast_to(scale, (8, 128))
    one_ref[...] = dot_rows(c0_ref[...], c1_ref[...])
    share = c1_ref[pl.ds(pl.multiple_of(spot_ref[0], 64), 64), :]
    two_ref[...] = dot_rows(share, c2_ref[...])


def tree_kernel(
    pivot_ref, spot_ref, gram_ref, scale_ref, right_one_ref, right_two_ref, c2_ref, o2_ref,
    inverse_ref, one_ref, two_ref, three_ref, root_ref,
    c3_ref, work,
):
    both = jnp.concatenate([c2_ref[...], o2_ref[...]], axis=0)
    c3_ref[...] = take_rows(pivot_ref[...], both)
    root_ref[...] = c3_ref[pl.ds(pl.multiple_of(spot_ref[2], 16), 16), :]
    scales = []
    for level in range(3):
        work[level] = gram_ref[level]
        scales.append(scale_ref[level, 0:1, 0:1])
    work[3], scale = scaled_gram(c3_ref[...])
    scales.append(scale)
    invert(work)
    share = c2_ref[pl.ds(pl.multiple_of(spot_ref[1], 32), 32), :]
    rights = (None, right_one_ref[...], right_two_ref[...], dot_rows(share, c3_ref[...]))
    outs = (inverse_ref, one_ref, two_ref, three_ref)
    eye = lax.broadcasted_iota(jnp.int32, (K, K), 0) == lax.broadcasted_iota(jnp.int32, (K, K), 1)
    for level in range(4):
        inverse = (jnp.where(eye, 2.0, 0.0) - work[level]) * scales[level]
        if level > 0:
            inverse = jnp.dot(
                rights[level],
                inverse,
                precision=lax.Precision.HIGHEST,
                preferred_element_type=F32,
            )
        outs[level][...] = inverse


def leaf_kernel(own_ref, a_ref, b_ref, c_ref, c0_ref, inverse_ref, out_ref):
    others = a_ref[...].astype(F32) + b_ref[...].astype(F32) + c_ref[...].astype(F32)
    right = dot_rows(own_ref[...] + others, c0_ref[...])
    out_ref[...] = jnp.dot(
        right, inverse_ref[...], precision=lax.Precision.HIGHEST, preferred_element_type=F32
    )


def body(targets, sources, omega, tree_order, leaf_pivots, pivots_one, pivots_two, pivots_three):
    y, x, z, k = (lax.axis_index(axis) for axis in ALL_AXES)
    leaf = ((y * NX + x) * NZ + z) * NK + k
    spots = [k * 64, ((z & 1) * 2 + k) * 32, ((z & 3) * 2 + k) * 16]
    spots = jnp.stack(spots).astype(jnp.int32)
    bits = (k, z & 1, (z >> 1) & 1)
    pivots = [
        lax.dynamic_index_in_dim(table, leaf >> level + 1, 0, keepdims=True)
        ^ (bits[level] * K).astype(jnp.int32)
        for level, table in enumerate((pivots_one, pivots_two, pivots_three))
    ]
    ahead = jnp.where(z & 1, 1, -1)
    me = jnp.stack([k] + [(z + d * ahead) & 7 for d in range(4)]).astype(jnp.int32)

    plane = pl.pallas_call(
        pack_kernel,
        out_shape=jax.ShapeDtypeStruct((NZ, 16, 128), F32),
        in_specs=[pl.BlockSpec(memory_space=pltpu.HBM)] * 3,
        out_specs=vmem(),
        scratch_shapes=[
            pltpu.VMEM((2, LEAF), F32),
            pltpu.VMEM((1, LEAF), jnp.int32),
            pltpu.VMEM((1, K), jnp.int32),
            pltpu.SemaphoreType.DMA((3,)),
        ],
        compiler_params=params(),
        name="pack",
    )(*(in_hbm(part) for part in (targets, tree_order.reshape(1, LEAF), leaf_pivots)))
    plane, omega = lax.optimization_barrier((plane, omega))
    plane = lax.all_to_all(plane, "z", split_axis=0, concat_axis=0, tiled=True)
    pad = jnp.zeros((14, sources.shape[1]), BF16)
    block = jnp.concatenate([omega, sources, pad], axis=0)
    plane, pivots, spots, me = lax.optimization_barrier((plane, pivots, spots, me))
    far = lax.ppermute(block, "z", [(s, s ^ 1) for s in range(NZ)])
    weights = [block, swap_cores(block)]
    features = source_features(*weights)
    table = copies_from(plane[:, :8].reshape(NZ * 8, 128), ("y", "x"), NY * NX)
    *leaves, chosen = target_features(me, table, swap_cores(table), plane[:, 8:])
    far, leaves, chosen = lax.optimization_barrier((far, leaves, chosen))
    far = [far, swap_cores(far)]

    def give(part, d):
        return lax.ppermute(part, ZK, along_z(d, True))

    (near,) = sketch_part(chosen, features, weights, [F32], finish=False)
    far_features = source_features(*far)
    c0, *parts = sketch_part(
        chosen, far_features, far, [F32] + [BF16] * 3, start=near
    )
    parts = [give(parts[d - 1], d) for d in (3, 2, 1)]
    weights, features = weights + far, features + far_features
    (third,) = sketch_part(leaves[3], features, weights, [BF16])
    third, parts = lax.optimization_barrier((third, parts))
    third = give(third, 3)
    c0 = c0 + (parts[0].astype(F32) + parts[1].astype(F32) + parts[2].astype(F32))
    c1 = choose(pivots[0], c0, swap_cores(c0))
    c1, leaf = lax.optimization_barrier((c1, leaves[2]))
    other1 = lax.ppermute(c1, "z", [(s, s ^ 1) for s in range(NZ)])
    (second,) = sketch_part(leaf, features, weights, [BF16])
    second, other1 = lax.optimization_barrier((second, other1))
    c2 = choose(pivots[1], c1, other1)
    c2, leaf = lax.optimization_barrier((c2, leaves[1]))
    other2 = lax.ppermute(c2, "z", [(s, s ^ 2) for s in range(NZ)])
    (first,) = sketch_part(leaf, features, weights, [BF16])
    own_leaf, first, second, third = lax.optimization_barrier((leaves[0], first, second, third))
    second = give(second, 2)
    (own,) = sketch_part(own_leaf, features, weights, [F32])
    own, first, other2, c0, c1, c2 = lax.optimization_barrier((own, first, other2, c0, c1, c2))
    first = give(first, 1)
    grams = pl.pallas_call(
        gram_kernel,
        out_shape=[
            jax.ShapeDtypeStruct((3, K, K), F32),
            jax.ShapeDtypeStruct((3, 8, 128), F32),
            jax.ShapeDtypeStruct((K, K), F32),
            jax.ShapeDtypeStruct((K // 2, K), F32),
        ],
        in_specs=[smem()] + [vmem()] * 3,
        out_specs=[vmem()] * 4,
        compiler_params=params(),
        name="grams",
    )(spots, c0, c1, c2)
    second, grams = lax.optimization_barrier((second, grams))
    inverse, one_out, two_out, three_out, root = pl.pallas_call(
        tree_kernel,
        out_shape=[
            jax.ShapeDtypeStruct((K, K), F32),
            jax.ShapeDtypeStruct((K, K), F32),
            jax.ShapeDtypeStruct((K // 2, K), F32),
            jax.ShapeDtypeStruct((K // 4, K), F32),
            jax.ShapeDtypeStruct((K // 8, S), F32),
        ],
        in_specs=[vmem(), smem()] + [vmem()] * 6,
        out_specs=[vmem()] * 5,
        scratch_shapes=[
            pltpu.VMEM((K, S), F32),
            pltpu.VMEM((4, K, K), F32),
        ],
        compiler_params=params(),
        name="tree",
    )(pivots[2], spots, *grams, c2, other2)
    leaf_out = pl.pallas_call(
        leaf_kernel,
        out_shape=jax.ShapeDtypeStruct((LEAF, K), F32),
        in_specs=[vmem()] * 6,
        out_specs=vmem(),
        compiler_params=params(),
        name="leaf_interp",
    )(own, third, second, first, c0, inverse)
    return leaf_out, one_out, two_out, three_out, root


def solution(mesh):
    finer = Mesh(mesh.devices.reshape(NY, NX, NZ, NK), ALL_AXES)
    col = ("z", "k")
    placed = (
        P(None, ALL_AXES),
        P(None, col),
        P(None, col),
        P(ALL_AXES),
        P(ALL_AXES, None),
        P(),
        P(),
        P(),
    )
    return jax.shard_map(
        body,
        mesh=finer,
        in_specs=placed,
        out_specs=(P(ALL_AXES, None),) * 5,
        check_vma=False,
    )
```
